32 devices in a mesh: slab: 8 (over z, y), mem: 4 (over x, core).
Axes of the slice: x: 2, y: 2, z: 4, core: 2. Of those that a mesh axis runs over, the one named last changes fastest.
Arguments:
- starting_states_set: float32 [128, 64, 1024], P('mem', 'slab'), may hold values from -6 to 6
- land_mask: int32 [64, 1024], P('slab'), may hold values 0 or 1
- cell_class: int32 [64, 1024], P('slab'), may hold values from 0 to 7
- kappa_table: float32 [8], replicated, may hold values from 0.08 to 0.2
- flow_table: float32 [2, 8], replicated, may hold values from -0.3 to 0.3
- obs_index: int32 [1024], P('slab'), may hold values from 0 to 8191
- obs_values: float32 [1024], P('slab'), may hold values from -24 to 24
- obs_var: float32 [1024], P('slab'), may hold values from 0.1 to 1
Outputs:
- analysis: float32 [128, 64, 1024], P('mem', 'slab')
The draws below stay inside these ranges and needn't reach their ends.
All inputs are finite; a program needn't handle non-finite values. No bound on the sum of `land_mask` on one device may be relied on, other than what follows from the above.
Results may differ from the reference program's by a relative error of at most 0.00016.
Values sent between devices are 32-bit elements; how exact they have to be, the bound alone decides.
A program may use at most 64 MiB of HBM per device.

```python
import math
import jax
import jax.numpy as jnp
from jax import lax

ENSEMBLE_SIZE = 128
EASTWARD_SPAN = 1024
LAT_DEV = 8
OBS_DEV = 128
STEPS = 8
ROOT_ITERATIONS = 8
NCLS = 8
NORTHWARD_SPAN = 64
NOBS = 1024
N_SLAB = 8


def plant(array, own_key, least, high):
    place = [jax.random.randint(jax.random.fold_in(own_key, axis), (), 0, length) for axis, length in enumerate(array.shape)]
    longest = array.shape.index(max(array.shape))
    neighbour = place[:longest] + [(place[longest] + 1) % array.shape[longest]] + place[longest + 1:]
    return array.at[tuple(place)].set(least).at[tuple(neighbour)].set(high)


def block_levels(rng, dims, split, smallest, top_value):
    level = 1.0
    for axis_at, parts in split:
        heights = jax.random.uniform(jax.random.fold_in(jax.random.fold_in(rng, 6), axis_at), (parts,), jnp.float32, smallest / len(split), top_value / len(split))
        level = level * jnp.repeat(jnp.exp(heights), dims[axis_at] // parts).reshape((-1,) + (1,) * (len(dims) - 1 - axis_at))
    return level


def noise(stream_key, shape, scale, bound, cuts=(), kind=jnp.bfloat16):
    result = jax.random.normal(stream_key, shape, jnp.float32) * scale
    if len(cuts) > 0:
        result = block_levels(stream_key, shape, cuts, -0.22, 0.18) * result
    return jnp.clip(result, min=-bound, max=bound).astype(kind)


def setup_inputs(seed: int = 0) -> dict:
    arg_keys = jax.random.split(jax.random.key(seed), 9)
    starting_states_set = noise(arg_keys[0], (ENSEMBLE_SIZE, NORTHWARD_SPAN, EASTWARD_SPAN), 1.0, 6.0, ((0, 4), (1, 8)), jnp.float32)
    land_mask = plant((jax.random.randint(arg_keys[1], (NORTHWARD_SPAN, EASTWARD_SPAN), 0, 8) < 7).astype(jnp.int32), jax.random.fold_in(arg_keys[1], 1), 0, 1)
    cell_class = plant(jax.random.randint(arg_keys[2], (NORTHWARD_SPAN, EASTWARD_SPAN), 0, NCLS), jax.random.fold_in(arg_keys[2], 1), 0, NCLS - 1).astype(jnp.int32)
    kappa_table = jnp.clip(jax.random.uniform(arg_keys[3], (NCLS,), jnp.float32, 0.08, 0.2), 0.08, 0.2)
    flow_table = jnp.clip(jax.random.uniform(arg_keys[4], (2, NCLS), jnp.float32, -0.3, 0.3), -0.3, 0.3)
    obs_index = plant(jax.random.randint(arg_keys[5], (NOBS,), 0, LAT_DEV * EASTWARD_SPAN), jax.random.fold_in(arg_keys[5], 1), 0, (LAT_DEV * EASTWARD_SPAN) - 1).astype(jnp.int32)
    obs_values = noise(arg_keys[6], (NOBS,), 4.0, 24.0, ((0, 8),), jnp.float32)
    obs_var = jnp.clip(jnp.exp(math.log(1.0) - 2.3025851 * jax.random.uniform(arg_keys[7], (NOBS,), jnp.float32) ** block_levels(arg_keys[7], (NOBS,), ((0, 8),), -0.2, 0.2)), 0.1, 1.0)
    return dict(starting_states_set=starting_states_set, land_mask=land_mask, cell_class=cell_class, kappa_table=kappa_table, flow_table=flow_table, obs_index=obs_index, obs_values=obs_values, obs_var=obs_var)


def advance(center, north, south, diffusion, flow_east, flow_north, wet_cells):
    edge = jnp.zeros_like(center[..., :1])
    east = jnp.concatenate([center[..., 1:], edge], axis=-1)
    west = jnp.concatenate([edge, center[..., :-1]], axis=-1)
    spread = north + south + east + west - 4.0 * center
    return wet_cells * (center + diffusion * spread - 0.5 * flow_east * (east - west) - 0.5 * flow_north * (north - south))

def reference(starting_states_set, land_mask, cell_class, kappa_table, flow_table, obs_index, obs_values, obs_var):
    highest = lax.Precision.HIGHEST
    diffusion = kappa_table[cell_class]
    flow_east = flow_table[0][cell_class]
    flow_north = flow_table[1][cell_class]
    wet_cells = land_mask.astype(jnp.float32)

    def single_prediction(current_profile):
        row_zero = jnp.zeros_like(current_profile[:1])
        for step in range(STEPS):
            north = jnp.concatenate([current_profile[1:], row_zero], axis=0)
            south = jnp.concatenate([row_zero, current_profile[:-1]], axis=0)
            current_profile = advance(current_profile, north, south, diffusion, flow_east, flow_north, wet_cells)
        return current_profile
    predictive_advance = lax.map(single_prediction, starting_states_set)
    raveled_vector = predictive_advance.reshape(ENSEMBLE_SIZE, NORTHWARD_SPAN * EASTWARD_SPAN)
    slab_of = jnp.arange(NOBS, dtype=jnp.int32) // OBS_DEV
    cells = slab_of * (LAT_DEV * EASTWARD_SPAN) + obs_index
    observed = jnp.take(raveled_vector, cells, axis=1)
    ybar = lax.optimization_barrier(jnp.sum(observed, axis=0)) / ENSEMBLE_SIZE
    factor = 1.0 + 2.0 * slab_of.astype(jnp.float32) / float(N_SLAB - 1)
    err = obs_var * factor
    anom = (observed - ybar) / jnp.sqrt(err * (ENSEMBLE_SIZE - 1.0))
    dev = (obs_values - ybar) / jnp.sqrt(err)
    gram = jnp.dot(anom, anom.T, precision=highest)
    proj = jnp.dot(anom, dev, precision=highest)
    ident = jnp.eye(ENSEMBLE_SIZE, dtype=jnp.float32)
    matrix = ident + gram
    scale = jnp.trace(matrix)
    upper = matrix / scale
    lower = ident
    for turn in range(ROOT_ITERATIONS):
        factor_q = 1.5 * ident - 0.5 * jnp.dot(lower, upper, precision=highest)
        upper = jnp.dot(upper, factor_q, precision=highest)
        lower = jnp.dot(factor_q, lower, precision=highest)
    transform_weights = lower / jnp.sqrt(scale)
    mean_w = jnp.dot(lower, jnp.dot(lower, proj, precision=highest), precision=highest) / (scale * jnp.sqrt(ENSEMBLE_SIZE - 1.0))
    total_w = transform_weights + mean_w[:, None]
    omega = 1.0 / ENSEMBLE_SIZE + total_w - (lax.optimization_barrier(jnp.sum(total_w, axis=0)) / ENSEMBLE_SIZE)[None, :]
    analysis = jnp.dot(omega.T, raveled_vector, precision=highest)
    return analysis.reshape(ENSEMBLE_SIZE, NORTHWARD_SPAN, EASTWARD_SPAN)
```

```python
import functools

import jax
import jax.numpy as jnp
from jax import lax
from jax.experimental import pallas as pl
from jax.experimental.pallas import tpu as pltpu
from jax.sharding import PartitionSpec as P

STEPS = 8
ROOT_ITERATIONS = 8
NCLS = 8
HEIGHT = 4
SPLIT = 4
PARTS = 2


def halves(x):
    high = x.astype(jnp.bfloat16)
    return high, (x - high.astype(jnp.float32)).astype(jnp.bfloat16)


def left_parts(x):
    high, low = halves(x)
    return jnp.concatenate([high, high, low], axis=1)


def right_parts(x):
    high, low = halves(x)
    return jnp.concatenate([high, low, high], axis=0)


def product(left, right):
    return jnp.dot(left, right, preferred_element_type=jnp.float32)


def dot(a, b):
    return product(left_parts(a), right_parts(b))


def cycle_kernel(
    n_slab, n_mem,
    states, classes_in, mask_in, kappa, flow, obs_index, obs_values, obs_var,
    out,
    buf, coef, geos, gobs, gval, pick, hxs, gpart, precv, gfull, turned, fore, mixed,
    geo_send, geo_recv, obs_send, obs_recv, y_send, y_recv, d_send, d_recv, r_send, r_recv, keep_sem,
    h_send, h_recv, p_send, p_recv, g_send, g_recv, a_send, a_recv, b_send, b_recv,
):
    s = lax.axis_index("slab")
    m = lax.axis_index("mem")
    q, y = lax.div(s, 2), lax.rem(s, 2)
    n_pair, n_group = n_slab // 2, 2 * n_mem
    octs, rows, lon = states.shape[0] // 2, states.shape[1], states.shape[3]
    half = lon // 2
    ens = fore.shape[1]
    n_obs = obs_index.shape[1]
    line, core = lax.div(m, 2), lax.rem(m, 2)
    sibling = 2 * line + 1 - core
    kd = octs * 16
    group = y * n_mem + m
    last = n_pair - 1
    step_pair = 2 * y - 1

    def device(pair, side, member):
        return (2 * pair + side, member)

    def remote(src, dst, send, recv, where):
        return pltpu.make_async_remote_copy(
            src_ref=src, dst_ref=dst, send_sem=send, recv_sem=recv,
            device_id=where, device_id_type=pl.DeviceIdType.MESH,
        )

    def peer(k):
        other = lax.rem(group + k, n_group)
        return other, lax.div(other, n_mem), lax.rem(other, n_mem)

    barrier = pltpu.get_barrier_semaphore()
    for k in range(1, n_group):
        _, ty, tm = peer(k)
        pl.semaphore_signal(barrier, inc=1, device_id=device(q, ty, tm), device_id_type=pl.DeviceIdType.MESH)
    for k in range(1, n_pair):
        tq = lax.rem(q + k, n_pair)
        pl.semaphore_signal(barrier, inc=1, device_id=device(tq, y, m), device_id_type=pl.DeviceIdType.MESH)
    pl.semaphore_wait(barrier, n_group - 1 + n_pair - 1)

    piece = 8 // SPLIT

    def y_copy(c, h):
        return remote(
            states.at[octs * (1 - y) + c, pl.ds(piece * h, piece)], buf.at[0, c, pl.ds(8 + 8 * y + piece * h, piece)],
            y_send.at[c, h], y_recv.at[c, h], device(q, 1 - y, m),
        )

    def y_wait(c, h):
        return remote(
            states.at[c, pl.ds(0, piece)], buf.at[0, c, pl.ds(16 - 8 * y + piece * h, piece)],
            y_send.at[c, h], y_recv.at[c, h], device(q, 1 - y, m),
        )

    def direct_copy(c):
        return remote(
            states.at[octs * y + c], buf.at[0, c, pl.ds(24 * (1 - y), 8)],
            d_send.at[c], d_recv.at[c], device(q + step_pair, y, m),
        )

    def relay_copy(c, h):
        return remote(
            buf.at[0, c, pl.ds(16 - 8 * y + piece * h, piece)], buf.at[0, c, pl.ds(24 * y + piece * h, piece)],
            r_send.at[c, h], r_recv.at[c, h], device(q - step_pair, y, m),
        )

    fields = (classes_in, mask_in)

    def geo_pair(f):
        return remote(
            fields[f], geos.at[1 + y, f], geo_send.at[0, f], geo_recv.at[1 + y, f], device(q, 1 - y, m)
        )

    def geo_direct(f):
        return remote(
            fields[f], geos.at[3 * (1 - y), f], geo_send.at[1, f], geo_recv.at[3 * (1 - y), f],
            device(q + step_pair, y, m),
        )

    def geo_relay(f):
        return remote(
            geos.at[2 - y, f], geos.at[3 * y, f], geo_send.at[2, f], geo_recv.at[3 * y, f],
            device(q - step_pair, y, m),
        )

    def geo_wait(slot, f):
        return remote(fields[f], geos.at[slot, f], geo_send.at[0, f], geo_recv.at[slot, f], device(q, 1 - y, m))

    observed = ((obs_index, gobs.at[y]), (obs_values, gval.at[y, 0]), (obs_var, gval.at[y, 1]))
    other_observed = ((obs_index, gobs.at[1 - y]), (obs_values, gval.at[1 - y, 0]), (obs_var, gval.at[1 - y, 1]))

    def obs_copy(f):
        return remote(observed[f][0], observed[f][1], obs_send.at[f], obs_recv.at[f], device(q, 1 - y, m))

    def obs_wait(f):
        return remote(other_observed[f][0], other_observed[f][1], obs_send.at[f], obs_recv.at[f], device(q, 1 - y, m))

    def keep(c):
        return pltpu.make_async_copy(states.at[octs * y + c], buf.at[0, c, pl.ds(8 + 8 * y, 8)], keep_sem.at[c])

    forward_edge = (q + step_pair >= 0) & (q + step_pair <= last)
    backward_edge = (q - step_pair >= 0) & (q - step_pair <= last)

    for f in range(2):
        geo_pair(f).start()
    for f in range(3):
        obs_copy(f).start()
    for c in range(octs):
        for h in range(SPLIT):
            y_copy(c, h).start()

    @pl.when(forward_edge)
    def _():
        for f in range(2):
            geo_direct(f).start()
        for c in range(octs):
            direct_copy(c).start()

    for c in range(octs):
        keep(c).start()
    for f in range(2):
        geos[1 + y, f] = fields[f][...]
    gobs[y] = obs_index[...]
    gval[y, 0] = obs_values[...]
    gval[y, 1] = obs_var[...]

    @pl.when(q == 0)
    def _():
        geos[0] = jnp.zeros(geos.shape[1:], jnp.int32)
        for c in range(octs):
            buf[0, c, 0:8] = jnp.zeros((8, 8, lon), jnp.float32)

    @pl.when(q == last)
    def _():
        geos[3] = jnp.zeros(geos.shape[1:], jnp.int32)
        for c in range(octs):
            buf[0, c, 24:32] = jnp.zeros((8, 8, lon), jnp.float32)

    for f in range(2):
        geo_wait(2 - y, f).wait_recv()

    @pl.when(backward_edge)
    def _():
        for f in range(2):
            geo_relay(f).start()
            geo_wait(3 * (1 - y), f).wait_recv()

    lane = lax.broadcasted_iota(jnp.int32, (8, lon), 1)

    def coefficients(k, carry):
        classes = geos[k, 0]
        wet = geos[k, 1].astype(jnp.float32)
        diffusion = jnp.zeros(classes.shape, jnp.float32)
        east = jnp.zeros(classes.shape, jnp.float32)
        north = jnp.zeros(classes.shape, jnp.float32)
        for label in range(NCLS):
            hit = classes == label
            diffusion = jnp.where(hit, kappa[label], diffusion)
            east = jnp.where(hit, flow[0, label], east)
            north = jnp.where(hit, flow[1, label], north)
        terms = (
            wet * (1.0 - 4.0 * diffusion),
            wet * (diffusion - 0.5 * north),
            wet * (diffusion + 0.5 * north),
            jnp.where(lane == lon - 1, 0.0, wet * (diffusion - 0.5 * east)),
            jnp.where(lane == 0, 0.0, wet * (diffusion + 0.5 * east)),
        )
        for index, term in enumerate(terms):
            for row in range(8):
                coef[8 * k + row, index] = jnp.broadcast_to(term[row : row + 1], (8, lon))
        return carry

    lax.fori_loop(1 - y, 4 - y, coefficients, 0)

    for f in range(3):
        obs_wait(f).wait_recv()
    place = jnp.concatenate([gobs[0], gobs[1]], axis=1)
    column = place & (lon - 1)
    pick[...] = jnp.where(
        lax.broadcasted_iota(jnp.int32, (lon, 2 * n_obs), 0) == column, 1.0, 0.0
    ).astype(jnp.bfloat16)
    side = lax.div(lax.broadcasted_iota(jnp.int32, (1, 2 * n_obs), 1), n_obs)
    obs_row = rows * side + (place >> (lon.bit_length() - 1))

    @pl.when(forward_edge)
    def _():
        for f in range(2):
            geo_wait(3 * y, f).wait_recv()

    lax.fori_loop(3 * y, 3 * y + 1, coefficients, 0)

    def relay(c, h):
        y_wait(c, h).wait_recv()

        @pl.when(backward_edge)
        def _():
            relay_copy(c, h).start()

    def advance(c, source, target, height, base):
        level = [buf[source, c, base - 1 + k] for k in range(height + 2)]
        fresh = []
        for k in range(height):
            center = level[k + 1]
            fresh.append(
                coef[base + k, 0] * center
                + coef[base + k, 1] * level[k + 2]
                + coef[base + k, 2] * level[k]
                + coef[base + k, 3] * pltpu.roll(center, lon - 1, 1)
                + coef[base + k, 4] * pltpu.roll(center, 1, 1)
            )
        for k in range(height):
            buf[target, c, base + k] = fresh[k]

    def buffers(pair_step, parity):
        if parity == 0:
            return jnp.where(pair_step == 0, 0, 2), 1
        return 1, 2

    def early(c):
        def two_steps(pair_step, carry):
            for parity in range(2):
                step = 2 * pair_step + parity + 1
                source, target = buffers(pair_step, parity)
                first = step + 8 * (1 - y)
                full = lax.div(24 - 2 * step, HEIGHT)

                def some(g, inner):
                    advance(c, source, target, HEIGHT, first + HEIGHT * g)
                    return inner

                lax.fori_loop(0, full, some, 0)
                if parity == 0:
                    advance(c, source, target, 2, first + 22 - 2 * step)
            return carry

        lax.fori_loop(0, STEPS // 2, two_steps, 0)

    def late(c):
        def two_steps(pair_step, carry):
            for parity in range(2):
                step = 2 * pair_step + parity + 1
                source, target = buffers(pair_step, parity)
                first = step + y * (24 - 2 * step)

                def some(g, inner):
                    advance(c, source, target, HEIGHT, first + HEIGHT * g)
                    return inner

                lax.fori_loop(0, 8 // HEIGHT, some, 0)
            return carry

        lax.fori_loop(0, STEPS // 2, two_steps, 0)

    def direct_arrived(c):
        keep(c).wait()

        @pl.when(backward_edge)
        def _():
            remote(states.at[c], buf.at[0, c, pl.ds(24 * (1 - y), 8)], d_send.at[c], d_recv.at[c], device(q, 1 - y, m)).wait_recv()

    def relay_arrived(c):
        @pl.when(forward_edge)
        def _():
            for h in range(SPLIT):
                remote(
                    states.at[c, pl.ds(0, piece)], buf.at[0, c, pl.ds(24 * y + piece * h, piece)],
                    r_send.at[c, h], r_recv.at[c, h], device(q, 1 - y, m),
                ).wait_recv()

    deep = rows // PARTS

    def a_copy(c, h, other, ty, tm):
        return remote(
            buf.at[2, c, pl.ds(8 + 8 * ty + deep * h, deep), :, pl.ds(pl.multiple_of(half * lax.rem(tm, 2), 128), half)],
            fore.at[pl.ds(deep * h, deep), pl.ds(pl.multiple_of(kd * m + 8 * octs * y + 8 * c, 8), 8), :],
            a_send.at[c, h, other], a_recv.at[c, h, group], device(q, ty, tm),
        )

    def a_wait(c, h, other, ty, tm):
        return remote(
            buf.at[2, c, pl.ds(8, deep), :, pl.ds(0, half)],
            fore.at[pl.ds(deep * h, deep), pl.ds(pl.multiple_of(kd * tm + 8 * octs * ty + 8 * c, 8), 8), :],
            a_send.at[c, h, other], a_recv.at[c, h, other], device(q, ty, tm),
        )

    def a_keep(c, h):
        return pltpu.make_async_copy(
            buf.at[2, c, pl.ds(8 + 8 * y + deep * h, deep), :, pl.ds(pl.multiple_of(half * core, 128), half)],
            fore.at[pl.ds(deep * h, deep), pl.ds(pl.multiple_of(kd * m + 8 * octs * y + 8 * c, 8), 8), :],
            a_send.at[c, h, group],
        )

    def a_start(c, h):
        for k in range(1, n_group):
            a_copy(c, h, *peer(k)).start()
        a_keep(c, h).start()

    own_rows = kd * m + 8 * octs * y

    def observe(c):
        rest = buf[2, c, 8:24].reshape(16 * 8, lon)
        pieces = []
        for _ in range(3):
            part = rest.astype(jnp.bfloat16)
            pieces.append(part)
            rest = rest - part.astype(jnp.float32)
        seen = jnp.dot(jnp.concatenate(pieces, axis=0), pick[...], preferred_element_type=jnp.float32)
        seen = seen[:128] + seen[128:256] + seen[256:]
        hx = jnp.zeros((8, 2 * n_obs), jnp.float32)
        for row in range(2 * rows):
            hx = hx + jnp.where(obs_row == row, seen[8 * row : 8 * row + 8], 0.0)
        hxs[pl.ds(pl.multiple_of(own_rows + 8 * c, 8), 8)] = hx

    for h in range(SPLIT):
        relay(0, h)
    direct_arrived(0)
    early(0)
    for c in range(octs):
        if c < octs - 1:
            for h in range(SPLIT // 2):
                relay(c + 1, h)
        relay_arrived(c)
        late(c)
        if c < octs - 1:
            a_start(c, 0)
            for h in range(SPLIT // 2, SPLIT):
                relay(c + 1, h)
            observe(c)
            direct_arrived(c + 1)
            early(c + 1)
    observe(octs - 1)

    mine = pl.ds(pl.multiple_of(own_rows, 8), 8 * octs)

    def h_copy(other, ty, tm):
        return remote(hxs.at[mine], hxs.at[mine], h_send.at[other], h_recv.at[group], device(q, ty, tm))

    def h_wait(other, ty, tm):
        there = hxs.at[pl.ds(pl.multiple_of(kd * tm + 8 * octs * ty, 8), 8 * octs)]
        return remote(there, there, h_send.at[other], h_recv.at[other], device(q, ty, tm))

    for k in range(1, n_group):
        h_copy(*peer(k)).start()
    for h in range(PARTS):
        for c in range(octs):
            if h > 0 or c == octs - 1:
                a_start(c, h)
    for k in range(1, n_group):
        h_wait(*peer(k)).wait_recv()

    share = ens // 2
    full = hxs[...]
    ybar = jnp.sum(full, axis=0, keepdims=True) / ens
    slab = (2 * q + side).astype(jnp.float32)
    err = jnp.concatenate([gval[0, 1], gval[1, 1]], axis=1) * (1.0 + 2.0 * slab / float(n_slab - 1))
    scaled = jnp.sqrt(err * (ens - 1.0))
    anom = (full - ybar) / scaled
    part = (hxs[pl.ds(pl.multiple_of(share * core, 8), share)] - ybar) / scaled
    dev = (jnp.concatenate([gval[0, 0], gval[1, 0]], axis=1) - ybar) / jnp.sqrt(err)
    both = jnp.concatenate([part, jnp.broadcast_to(dev, (16, 2 * n_obs))], axis=0)
    high, low = halves(anom)
    sums = lax.dot_general(
        left_parts(both), jnp.concatenate([high, low, high], axis=1), (((1,), (1,)), ((), ())),
        preferred_element_type=jnp.float32,
    )
    gpart[...] = sums[: share + 8]

    def p_copy(k):
        tq = lax.rem(q + k, n_pair)
        return remote(gpart, precv.at[q], p_send.at[tq], p_recv.at[q], device(tq, y, m))

    def p_wait(k):
        tq = lax.rem(q + k, n_pair)
        return remote(gpart, precv.at[tq], p_send.at[tq], p_recv.at[tq], device(tq, y, m))

    for k in range(1, n_pair):
        p_copy(k).start()
    precv[q] = sums[: share + 8]
    for k in range(1, n_pair):
        p_wait(k).wait_recv()
    total = precv[0]
    for k in range(1, n_pair):
        total = total + precv[k]
    own = pl.ds(pl.multiple_of(share * core, 8), share)
    theirs = pl.ds(pl.multiple_of(share * (1 - core), 8), share)
    gfull[own] = total[:share]
    g_copy = remote(gfull.at[own], gfull.at[own], g_send, g_recv, device(q, y, sibling))
    g_copy.start()
    proj = jnp.concatenate([total[share:], total[share:]], axis=0)
    remote(gfull.at[theirs], gfull.at[theirs], g_send, g_recv, device(q, y, sibling)).wait_recv()

    ident = jnp.where(
        lax.broadcasted_iota(jnp.int32, (ens, ens), 0) == lax.broadcasted_iota(jnp.int32, (ens, ens), 1), 1.0, 0.0
    )
    matrix = ident + gfull[...]
    scale = jnp.sum(jnp.sum(matrix * ident, axis=1, keepdims=True), axis=0, keepdims=True)

    upper = matrix / scale
    factor = 1.5 * ident - 0.5 * upper
    upper, lower = dot(upper, factor), factor
    for turn in range(ROOT_ITERATIONS - 1):
        factor = 1.5 * ident - 0.5 * dot(lower, upper)
        if turn < ROOT_ITERATIONS - 2:
            upper = dot(upper, factor)
        lower = dot(factor, lower)
    high, low = halves(proj)
    once = lax.dot_general(
        left_parts(lower), jnp.concatenate([high, low, high], axis=1), (((1,), (1,)), ((), ())),
        preferred_element_type=jnp.float32,
    )
    mean_w = dot(lower, once)[:, :1] / (scale * jnp.sqrt(jnp.float32(ens - 1.0)))
    total_w = lower / jnp.sqrt(scale) + mean_w
    omega = 1.0 / ens + total_w - jnp.sum(total_w, axis=0, keepdims=True) / ens
    turned[...] = omega.T
    weights = left_parts(
        jnp.concatenate(
            [turned[pl.ds(pl.multiple_of(kd * m, 8), kd)], turned[pl.ds(pl.multiple_of(kd * sibling, 8), kd)]], axis=0
        )
    )

    def b_copy(h):
        return remote(
            mixed.at[pl.ds(deep * h, deep)],
            out.at[pl.ds(deep * h, deep), :, pl.ds(pl.multiple_of(half * core, 128), half)],
            b_send.at[h], b_recv.at[h], device(q, y, sibling),
        )

    def b_wait(h):
        return remote(
            mixed.at[pl.ds(deep * h, deep)],
            out.at[pl.ds(deep * h, deep), :, pl.ds(pl.multiple_of(half * (1 - core), 128), half)],
            b_send.at[h], b_recv.at[h], device(q, y, sibling),
        )

    for h in range(PARTS):
        for c in range(octs):
            a_keep(c, h).wait()
            for k in range(1, n_group):
                a_wait(c, h, *peer(k)).wait_recv()
        for row in range(deep * h, deep * h + deep):
            result = product(weights, right_parts(fore[row]))
            mixed[row] = result[kd:]
            out[row, :, pl.ds(pl.multiple_of(half * core, 128), half)] = result[:kd]
        b_copy(h).start()

    for f in range(2):
        geo_pair(f).wait_send()
    for f in range(3):
        obs_copy(f).wait_send()
    for c in range(octs):
        for h in range(SPLIT):
            y_copy(c, h).wait_send()

    @pl.when(forward_edge)
    def _():
        for f in range(2):
            geo_direct(f).wait_send()
        for c in range(octs):
            direct_copy(c).wait_send()

    @pl.when(backward_edge)
    def _():
        for f in range(2):
            geo_relay(f).wait_send()
        for c in range(octs):
            for h in range(SPLIT):
                relay_copy(c, h).wait_send()

    for k in range(1, n_group):
        for c in range(octs):
            for h in range(PARTS):
                a_copy(c, h, *peer(k)).wait_send()
        h_copy(*peer(k)).wait_send()
    for k in range(1, n_pair):
        p_copy(k).wait_send()
    g_copy.wait_send()
    for h in range(PARTS):
        b_copy(h).wait_send()
        b_wait(h).wait_recv()


def local(n_slab, n_mem, states, land_mask, cell_class, kappa, flow, obs_index, obs_values, obs_var):
    kd, rows, lon = states.shape
    ens = kd * n_mem
    n_pair, n_group, octs = n_slab // 2, 2 * n_mem, kd // 16
    n_obs = obs_index.shape[0]
    swapped = states.reshape(kd // 8, 8, rows, lon).transpose(0, 2, 1, 3)
    dma = pltpu.SemaphoreType.DMA
    vmem = pl.BlockSpec(memory_space=pltpu.VMEM)
    smem = pl.BlockSpec(memory_space=pltpu.SMEM)
    f32 = jnp.float32
    out = pl.pallas_call(
        functools.partial(cycle_kernel, n_slab, n_mem),
        out_shape=jax.ShapeDtypeStruct((rows, kd, lon), f32),
        in_specs=[vmem, vmem, vmem, smem, smem, vmem, vmem, vmem],
        out_specs=vmem,
        scratch_shapes=[
            pltpu.VMEM((3, octs, 4 * rows, 8, lon), f32),
            pltpu.VMEM((4 * rows, 5, 8, lon), f32),
            pltpu.VMEM((4, 2, rows, lon), jnp.int32),
            pltpu.VMEM((2, 1, n_obs), jnp.int32),
            pltpu.VMEM((2, 2, 1, n_obs), f32),
            pltpu.VMEM((lon, 2 * n_obs), jnp.bfloat16),
            pltpu.VMEM((ens, 2 * n_obs), f32),
            pltpu.VMEM((ens // 2 + 8, ens), f32),
            pltpu.VMEM((n_pair, ens // 2 + 8, ens), f32),
            pltpu.VMEM((ens, ens), f32),
            pltpu.VMEM((ens, ens), f32),
            pltpu.VMEM((rows, ens, lon // 2), f32),
            pltpu.VMEM((rows, kd, lon // 2), f32),
            dma((3, 2)), dma((4, 2)), dma((3,)), dma((3,)), dma((octs, SPLIT)), dma((octs, SPLIT)),
            dma((octs,)), dma((octs,)), dma((octs, SPLIT)), dma((octs, SPLIT)), dma((octs,)),
            dma((n_group,)), dma((n_group,)), dma((n_pair,)), dma((n_pair,)), dma, dma,
            dma((octs, PARTS, n_group)), dma((octs, PARTS, n_group)), dma((PARTS,)), dma((PARTS,)),
        ],
        compiler_params=pltpu.CompilerParams(
            collective_id=0, has_side_effects=True, vmem_limit_bytes=48 * 1024 * 1024
        ),
        name="cycle",
    )(
        swapped, cell_class, land_mask, kappa, flow,
        obs_index.reshape(1, n_obs), obs_values.reshape(1, n_obs), obs_var.reshape(1, n_obs),
    )
    return out.transpose(1, 0, 2)


def solution(mesh):
    return jax.shard_map(
        functools.partial(local, mesh.shape["slab"], mesh.shape["mem"]),
        mesh=mesh,
        in_specs=(
            P("mem", "slab", None),
            P("slab", None),
            P("slab", None),
            P(),
            P(),
            P("slab"),
            P("slab"),
            P("slab"),
        ),
        out_specs=P("mem", "slab", None),
        check_vma=False,
    )
```

```python
import functools

import jax
import jax.numpy as jnp
from jax import lax
from jax.experimental import pallas as pl
from jax.experimental.pallas import tpu as pltpu
from jax.sharding import PartitionSpec as P

STEPS = 8
ROOT_ITERATIONS = 8
NCLS = 8
HEIGHT = 4
SPLIT = 4
PARTS = 2


def halves(x):
    high = x.astype(jnp.bfloat16)
    return high, (x - high.astype(jnp.float32)).astype(jnp.bfloat16)


def left_parts(x):
    high, low = halves(x)
    return jnp.concatenate([high, high, low], axis=1)


def right_parts(x):
    high, low = halves(x)
    return jnp.concatenate([high, low, high], axis=0)


def product(left, right):
    return jnp.dot(left, right, preferred_element_type=jnp.float32)


def dot(a, b):
    return product(left_parts(a), right_parts(b))


def cycle_kernel(
    n_slab, n_mem,
    states, classes_in, mask_in, kappa, flow, obs_index, obs_values, obs_var,
    out,
    buf, coef, geos, gobs, gval, pick, hxs, gpart, precv, gfull, turned, fore, mixed,
    geo_send, geo_recv, obs_send, obs_recv, y_send, y_recv, d_send, d_recv, r_send, r_recv, keep_sem,
    h_send, h_recv, p_send, p_recv, g_send, g_recv, a_send, a_recv, b_send, b_recv,
):
    s = lax.axis_index("slab")
    m = lax.axis_index("mem")
    q, y = lax.div(s, 2), lax.rem(s, 2)
    n_pair, n_group = n_slab // 2, 2 * n_mem
    octs, rows, lon = states.shape[0] // 2, states.shape[1], states.shape[3]
    half = lon // 2
    ens = fore.shape[1]
    n_obs = obs_index.shape[1]
    line, core = lax.div(m, 2), lax.rem(m, 2)
    sibling = 2 * line + 1 - core
    kd = octs * 16
    group = y * n_mem + m
    last = n_pair - 1
    step_pair = 2 * y - 1

    def device(pair, side, member):
        return (2 * pair + side, member)

    def remote(src, dst, send, recv, where):
        return pltpu.make_async_remote_copy(
            src_ref=src, dst_ref=dst, send_sem=send, recv_sem=recv,
            device_id=where, device_id_type=pl.DeviceIdType.MESH,
        )

    def peer(k):
        other = lax.rem(group + k, n_group)
        return other, lax.div(other, n_mem), lax.rem(other, n_mem)

    barrier = pltpu.get_barrier_semaphore()
    for k in range(1, n_group):
        _, ty, tm = peer(k)
        pl.semaphore_signal(barrier, inc=1, device_id=device(q, ty, tm), device_id_type=pl.DeviceIdType.MESH)
    for k in range(1, n_pair):
        tq = lax.rem(q + k, n_pair)
        pl.semaphore_signal(barrier, inc=1, device_id=device(tq, y, m), device_id_type=pl.DeviceIdType.MESH)
    pl.semaphore_wait(barrier, n_group - 1 + n_pair - 1)

    piece = 8 // SPLIT

    def y_copy(c, h):
        return remote(
            states.at[octs * (1 - y) + c, pl.ds(piece * h, piece)], buf.at[0, c, pl.ds(8 + 8 * y + piece * h, piece)],
            y_send.at[c, h], y_recv.at[c, h], device(q, 1 - y, m),
        )

    def y_wait(c, h):
        return remote(
            states.at[c, pl.ds(0, piece)], buf.at[0, c, pl.ds(16 - 8 * y + piece * h, piece)],
            y_send.at[c, h], y_recv.at[c, h], device(q, 1 - y, m),
        )

    def direct_copy(c):
        return remote(
            states.at[octs * y + c], buf.at[0, c, pl.ds(24 * (1 - y), 8)],
            d_send.at[c], d_recv.at[c], device(q + step_pair, y, m),
        )

    def relay_copy(c, h):
        return remote(
            buf.at[0, c, pl.ds(16 - 8 * y + piece * h, piece)], buf.at[0, c, pl.ds(24 * y + piece * h, piece)],
            r_send.at[c, h], r_recv.at[c, h], device(q - step_pair, y, m),
        )

    fields = (classes_in, mask_in)

    def geo_pair(f):
        return remote(
            fields[f], geos.at[1 + y, f], geo_send.at[0, f], geo_recv.at[1 + y, f], device(q, 1 - y, m)
        )

    def geo_direct(f):
        return remote(
            fields[f], geos.at[3 * (1 - y), f], geo_send.at[1, f], geo_recv.at[3 * (1 - y), f],
            device(q + step_pair, y, m),
        )

    def geo_relay(f):
        return remote(
            geos.at[2 - y, f], geos.at[3 * y, f], geo_send.at[2, f], geo_recv.at[3 * y, f],
            device(q - step_pair, y, m),
        )

    def geo_wait(slot, f):
        return remote(fields[f], geos.at[slot, f], geo_send.at[0, f], geo_recv.at[slot, f], device(q, 1 - y, m))

    observed = ((obs_index, gobs.at[y]), (obs_values, gval.at[y, 0]), (obs_var, gval.at[y, 1]))
    other_observed = ((obs_index, gobs.at[1 - y]), (obs_values, gval.at[1 - y, 0]), (obs_var, gval.at[1 - y, 1]))

    def obs_copy(f):
        return remote(observed[f][0], observed[f][1], obs_send.at[f], obs_recv.at[f], device(q, 1 - y, m))

    def obs_wait(f):
        return remote(other_observed[f][0], other_observed[f][1], obs_send.at[f], obs_recv.at[f], device(q, 1 - y, m))

    def keep(c):
        return pltpu.make_async_copy(states.at[octs * y + c], buf.at[0, c, pl.ds(8 + 8 * y, 8)], keep_sem.at[c])

    forward_edge = (q + step_pair >= 0) & (q + step_pair <= last)
    backward_edge = (q - step_pair >= 0) & (q - step_pair <= last)

    for f in range(2):
        geo_pair(f).start()
    for f in range(3):
        obs_copy(f).start()
    for c in range(octs):
        for h in range(SPLIT):
            y_copy(c, h).start()

    @pl.when(forward_edge)
    def _():
        for f in range(2):
            geo_direct(f).start()
        for c in range(octs):
            direct_copy(c).start()

    for c in range(octs):
        keep(c).start()
    for f in range(2):
        geos[1 + y, f] = fields[f][...]
    gobs[y] = obs_index[...]
    gval[y, 0] = obs_values[...]
    gval[y, 1] = obs_var[...]

    @pl.when(q == 0)
    def _():
        geos[0] = jnp.zeros(geos.shape[1:], jnp.int32)
        for c in range(octs):
            buf[0, c, 0:8] = jnp.zeros((8, 8, lon), jnp.float32)

    @pl.when(q == last)
    def _():
        geos[3] = jnp.zeros(geos.shape[1:], jnp.int32)
        for c in range(octs):
            buf[0, c, 24:32] = jnp.zeros((8, 8, lon), jnp.float32)

    for f in range(2):
        geo_wait(2 - y, f).wait_recv()

    @pl.when(backward_edge)
    def _():
        for f in range(2):
            geo_relay(f).start()
            geo_wait(3 * (1 - y), f).wait_recv()

    lane = lax.broadcasted_iota(jnp.int32, (8, lon), 1)

    def coefficients(k, carry):
        classes = geos[k, 0]
        wet = geos[k, 1].astype(jnp.float32)
        diffusion = jnp.zeros(classes.shape, jnp.float32)
        east = jnp.zeros(classes.shape, jnp.float32)
        north = jnp.zeros(classes.shape, jnp.float32)
        for label in range(NCLS):
            hit = classes == label
            diffusion = jnp.where(hit, kappa[label], diffusion)
            east = jnp.where(hit, flow[0, label], east)
            north = jnp.where(hit, flow[1, label], north)
        terms = (
            wet * (1.0 - 4.0 * diffusion),
            wet * (diffusion - 0.5 * north),
            wet * (diffusion + 0.5 * north),
            jnp.where(lane == lon - 1, 0.0, wet * (diffusion - 0.5 * east)),
            jnp.where(lane == 0, 0.0, wet * (diffusion + 0.5 * east)),
        )
        for index, term in enumerate(terms):
            for row in range(8):
                coef[8 * k + row, index] = jnp.broadcast_to(term[row : row + 1], (8, lon))
        return carry

    lax.fori_loop(1 - y, 4 - y, coefficients, 0)

    for f in range(3):
        obs_wait(f).wait_recv()
    place = jnp.concatenate([gobs[0], gobs[1]], axis=1)
    column = place & (lon - 1)
    pick[...] = jnp.where(
        lax.broadcasted_iota(jnp.int32, (lon, 2 * n_obs), 0) == column, 1.0, 0.0
    ).astype(jnp.bfloat16)
    side = lax.div(lax.broadcasted_iota(jnp.int32, (1, 2 * n_obs), 1), n_obs)
    obs_row = rows * side + (place >> (lon.bit_length() - 1))

    @pl.when(forward_edge)
    def _():
        for f in range(2):
            geo_wait(3 * y, f).wait_recv()

    lax.fori_loop(3 * y, 3 * y + 1, coefficients, 0)

    def relay(c, h):
        y_wait(c, h).wait_recv()

        @pl.when(backward_edge)
        def _():
            relay_copy(c, h).start()

    def advance(c, source, target, height, base):
        level = [buf[source, c, base - 1 + k] for k in range(height + 2)]
        fresh = []
        for k in range(height):
            center = level[k + 1]
            fresh.append(
                coef[base + k, 0] * center
                + coef[base + k, 1] * level[k + 2]
                + coef[base + k, 2] * level[k]
                + coef[base + k, 3] * pltpu.roll(center, lon - 1, 1)
                + coef[base + k, 4] * pltpu.roll(center, 1, 1)
            )
        for k in range(height):
            buf[target, c, base + k] = fresh[k]

    def buffers(pair_step, parity):
        if parity == 0:
            return jnp.where(pair_step == 0, 0, 2), 1
        return 1, 2

    def early(c):
        def two_steps(pair_step, carry):
            for parity in range(2):
                step = 2 * pair_step + parity + 1
                source, target = buffers(pair_step, parity)
                first = step + 8 * (1 - y)
                full = lax.div(24 - 2 * step, HEIGHT)

                def some(g, inner):
                    advance(c, source, target, HEIGHT, first + HEIGHT * g)
                    return inner

                lax.fori_loop(0, full, some, 0)
                if parity == 0:
                    advance(c, source, target, 2, first + 22 - 2 * step)
            return carry

        lax.fori_loop(0, STEPS // 2, two_steps, 0)

    def late(c):
        def two_steps(pair_step, carry):
            for parity in range(2):
                step = 2 * pair_step + parity + 1
                source, target = buffers(pair_step, parity)
                first = step + y * (24 - 2 * step)

                def some(g, inner):
                    advance(c, source, target, HEIGHT, first + HEIGHT * g)
                    return inner

                lax.fori_loop(0, 8 // HEIGHT, some, 0)
            return carry

        lax.fori_loop(0, STEPS // 2, two_steps, 0)

    def direct_arrived(c):
        keep(c).wait()

        @pl.when(backward_edge)
        def _():
            remote(states.at[c], buf.at[0, c, pl.ds(24 * (1 - y), 8)], d_send.at[c], d_recv.at[c], device(q, 1 - y, m)).wait_recv()

    def relay_arrived(c):
        @pl.when(forward_edge)
        def _():
            for h in range(SPLIT):
                remote(
                    states.at[c, pl.ds(0, piece)], buf.at[0, c, pl.ds(24 * y + piece * h, piece)],
                    r_send.at[c, h], r_recv.at[c, h], device(q, 1 - y, m),
                ).wait_recv()

    deep = rows // PARTS

    def a_copy(c, h, other, ty, tm):
        return remote(
            buf.at[2, c, pl.ds(8 + 8 * ty + deep * h, deep), :, pl.ds(pl.multiple_of(half * lax.rem(tm, 2), 128), half)],
            fore.at[pl.ds(deep * h, deep), pl.ds(pl.multiple_of(kd * m + 8 * octs * y + 8 * c, 8), 8), :],
            a_send.at[c, h, other], a_recv.at[c, h, group], device(q, ty, tm),
        )

    def a_wait(c, h, other, ty, tm):
        return remote(
            buf.at[2, c, pl.ds(8, deep), :, pl.ds(0, half)],
            fore.at[pl.ds(deep * h, deep), pl.ds(pl.multiple_of(kd * tm + 8 * octs * ty + 8 * c, 8), 8), :],
            a_send.at[c, h, other], a_recv.at[c, h, other], device(q, ty, tm),
        )

    def a_keep(c, h):
        return pltpu.make_async_copy(
            buf.at[2, c, pl.ds(8 + 8 * y + deep * h, deep), :, pl.ds(pl.multiple_of(half * core, 128), half)],
            fore.at[pl.ds(deep * h, deep), pl.ds(pl.multiple_of(kd * m + 8 * octs * y + 8 * c, 8), 8), :],
            a_send.at[c, h, group],
        )

    def far_start(c, h):
        for k in range(n_mem):
            tm = lax.rem(m + 2 + k, n_mem)
            a_copy(c, h, (1 - y) * n_mem + tm, 1 - y, tm).start()

    def near_start(c, h):
        for k in range(1, n_mem):
            tm = lax.rem(m + k, n_mem)
            a_copy(c, h, y * n_mem + tm, y, tm).start()
        a_keep(c, h).start()

    own_rows = kd * m + 8 * octs * y

    def observe(c):
        rest = buf[2, c, 8:24].reshape(16 * 8, lon)
        pieces = []
        for _ in range(3):
            part = rest.astype(jnp.bfloat16)
            pieces.append(part)
            rest = rest - part.astype(jnp.float32)
        seen = jnp.dot(jnp.concatenate(pieces, axis=0), pick[...], preferred_element_type=jnp.float32)
        seen = seen[:128] + seen[128:256] + seen[256:]
        hx = jnp.zeros((8, 2 * n_obs), jnp.float32)
        for row in range(2 * rows):
            hx = hx + jnp.where(obs_row == row, seen[8 * row : 8 * row + 8], 0.0)
        hxs[pl.ds(pl.multiple_of(own_rows + 8 * c, 8), 8)] = hx

    for h in range(SPLIT):
        relay(0, h)
    direct_arrived(0)
    early(0)
    far_start(0, 0)
    for c in range(octs):
        if c < octs - 1:
            for h in range(SPLIT // 2):
                relay(c + 1, h)
        relay_arrived(c)
        late(c)
        if c < octs - 1:
            for h in range(PARTS):
                near_start(c, h)
            for h in range(SPLIT // 2, SPLIT):
                relay(c + 1, h)
            direct_arrived(c + 1)
            early(c + 1)
            observe(c)
    observe(octs - 1)

    mine = pl.ds(pl.multiple_of(own_rows, 8), 8 * octs)

    def h_copy(other, ty, tm):
        return remote(hxs.at[mine], hxs.at[mine], h_send.at[other], h_recv.at[group], device(q, ty, tm))

    def h_wait(other, ty, tm):
        there = hxs.at[pl.ds(pl.multiple_of(kd * tm + 8 * octs * ty, 8), 8 * octs)]
        return remote(there, there, h_send.at[other], h_recv.at[other], device(q, ty, tm))

    for k in range(1, n_group):
        h_copy(*peer(k)).start()
    for h in range(PARTS):
        for c in range(octs):
            if h > 0 or c > 0:
                far_start(c, h)
        for c in range(1, octs):
            near_start(c, h)
    for k in range(1, n_group):
        h_wait(*peer(k)).wait_recv()

    share = ens // 2
    full = hxs[...]
    ybar = jnp.sum(full, axis=0, keepdims=True) / ens
    slab = (2 * q + side).astype(jnp.float32)
    err = jnp.concatenate([gval[0, 1], gval[1, 1]], axis=1) * (1.0 + 2.0 * slab / float(n_slab - 1))
    scaled = jnp.sqrt(err * (ens - 1.0))
    anom = (full - ybar) / scaled
    part = (hxs[pl.ds(pl.multiple_of(share * core, 8), share)] - ybar) / scaled
    dev = (jnp.concatenate([gval[0, 0], gval[1, 0]], axis=1) - ybar) / jnp.sqrt(err)
    both = jnp.concatenate([part, jnp.broadcast_to(dev, (16, 2 * n_obs))], axis=0)
    high, low = halves(anom)
    sums = lax.dot_general(
        left_parts(both), jnp.concatenate([high, low, high], axis=1), (((1,), (1,)), ((), ())),
        preferred_element_type=jnp.float32,
    )
    gpart[...] = sums[: share + 8]

    def p_copy(k):
        tq = lax.rem(q + k, n_pair)
        return remote(gpart, precv.at[q], p_send.at[tq], p_recv.at[q], device(tq, y, m))

    def p_wait(k):
        tq = lax.rem(q + k, n_pair)
        return remote(gpart, precv.at[tq], p_send.at[tq], p_recv.at[tq], device(tq, y, m))

    for k in range(1, n_pair):
        p_copy(k).start()
    precv[q] = sums[: share + 8]
    for k in range(1, n_pair):
        p_wait(k).wait_recv()
    total = precv[0]
    for k in range(1, n_pair):
        total = total + precv[k]
    own = pl.ds(pl.multiple_of(share * core, 8), share)
    theirs = pl.ds(pl.multiple_of(share * (1 - core), 8), share)
    gfull[own] = total[:share]
    g_copy = remote(gfull.at[own], gfull.at[own], g_send, g_recv, device(q, y, sibling))
    g_copy.start()
    proj = jnp.concatenate([total[share:], total[share:]], axis=0)
    remote(gfull.at[theirs], gfull.at[theirs], g_send, g_recv, device(q, y, sibling)).wait_recv()

    ident = jnp.where(
        lax.broadcasted_iota(jnp.int32, (ens, ens), 0) == lax.broadcasted_iota(jnp.int32, (ens, ens), 1), 1.0, 0.0
    )
    matrix = ident + gfull[...]
    scale = jnp.sum(jnp.sum(matrix * ident, axis=1, keepdims=True), axis=0, keepdims=True)

    upper = matrix / scale
    factor = 1.5 * ident - 0.5 * upper
    upper, lower = dot(upper, factor), factor
    for turn in range(ROOT_ITERATIONS - 1):
        factor = 1.5 * ident - 0.5 * dot(lower, upper)
        if turn < ROOT_ITERATIONS - 2:
            upper = dot(upper, factor)
        lower = dot(factor, lower)
    high, low = halves(proj)
    once = lax.dot_general(
        left_parts(lower), jnp.concatenate([high, low, high], axis=1), (((1,), (1,)), ((), ())),
        preferred_element_type=jnp.float32,
    )
    mean_w = dot(lower, once)[:, :1] / (scale * jnp.sqrt(jnp.float32(ens - 1.0)))
    total_w = lower / jnp.sqrt(scale) + mean_w
    omega = 1.0 / ens + total_w - jnp.sum(total_w, axis=0, keepdims=True) / ens
    turned[...] = omega.T
    weights = left_parts(
        jnp.concatenate(
            [turned[pl.ds(pl.multiple_of(kd * m, 8), kd)], turned[pl.ds(pl.multiple_of(kd * sibling, 8), kd)]], axis=0
        )
    )

    def b_copy(h):
        return remote(
            mixed.at[pl.ds(deep * h, deep)],
            out.at[pl.ds(deep * h, deep), :, pl.ds(pl.multiple_of(half * core, 128), half)],
            b_send.at[h], b_recv.at[h], device(q, y, sibling),
        )

    def b_wait(h):
        return remote(
            mixed.at[pl.ds(deep * h, deep)],
            out.at[pl.ds(deep * h, deep), :, pl.ds(pl.multiple_of(half * (1 - core), 128), half)],
            b_send.at[h], b_recv.at[h], device(q, y, sibling),
        )

    for h in range(PARTS):
        for c in range(octs):
            a_keep(c, h).wait()
            for k in range(1, n_group):
                a_wait(c, h, *peer(k)).wait_recv()
        for row in range(deep * h, deep * h + deep):
            result = product(weights, right_parts(fore[row]))
            mixed[row] = result[kd:]
            out[row, :, pl.ds(pl.multiple_of(half * core, 128), half)] = result[:kd]
        b_copy(h).start()

    for f in range(2):
        geo_pair(f).wait_send()
    for f in range(3):
        obs_copy(f).wait_send()
    for c in range(octs):
        for h in range(SPLIT):
            y_copy(c, h).wait_send()

    @pl.when(forward_edge)
    def _():
        for f in range(2):
            geo_direct(f).wait_send()
        for c in range(octs):
            direct_copy(c).wait_send()

    @pl.when(backward_edge)
    def _():
        for f in range(2):
            geo_relay(f).wait_send()
        for c in range(octs):
            for h in range(SPLIT):
                relay_copy(c, h).wait_send()

    for k in range(1, n_group):
        for c in range(octs):
            for h in range(PARTS):
                a_copy(c, h, *peer(k)).wait_send()
        h_copy(*peer(k)).wait_send()
    for k in range(1, n_pair):
        p_copy(k).wait_send()
    g_copy.wait_send()
    for h in range(PARTS):
        b_copy(h).wait_send()
        b_wait(h).wait_recv()


def local(n_slab, n_mem, states, land_mask, cell_class, kappa, flow, obs_index, obs_values, obs_var):
    kd, rows, lon = states.shape
    ens = kd * n_mem
    n_pair, n_group, octs = n_slab // 2, 2 * n_mem, kd // 16
    n_obs = obs_index.shape[0]
    swapped = states.reshape(kd // 8, 8, rows, lon).transpose(0, 2, 1, 3)
    dma = pltpu.SemaphoreType.DMA
    vmem = pl.BlockSpec(memory_space=pltpu.VMEM)
    smem = pl.BlockSpec(memory_space=pltpu.SMEM)
    f32 = jnp.float32
    out = pl.pallas_call(
        functools.partial(cycle_kernel, n_slab, n_mem),
        out_shape=jax.ShapeDtypeStruct((rows, kd, lon), f32),
        in_specs=[vmem, vmem, vmem, smem, smem, vmem, vmem, vmem],
        out_specs=vmem,
        scratch_shapes=[
            pltpu.VMEM((3, octs, 4 * rows, 8, lon), f32),
            pltpu.VMEM((4 * rows, 5, 8, lon), f32),
            pltpu.VMEM((4, 2, rows, lon), jnp.int32),
            pltpu.VMEM((2, 1, n_obs), jnp.int32),
            pltpu.VMEM((2, 2, 1, n_obs), f32),
            pltpu.VMEM((lon, 2 * n_obs), jnp.bfloat16),
            pltpu.VMEM((ens, 2 * n_obs), f32),
            pltpu.VMEM((ens // 2 + 8, ens), f32),
            pltpu.VMEM((n_pair, ens // 2 + 8, ens), f32),
            pltpu.VMEM((ens, ens), f32),
            pltpu.VMEM((ens, ens), f32),
            pltpu.VMEM((rows, ens, lon // 2), f32),
            pltpu.VMEM((rows, kd, lon // 2), f32),
            dma((3, 2)), dma((4, 2)), dma((3,)), dma((3,)), dma((octs, SPLIT)), dma((octs, SPLIT)),
            dma((octs,)), dma((octs,)), dma((octs, SPLIT)), dma((octs, SPLIT)), dma((octs,)),
            dma((n_group,)), dma((n_group,)), dma((n_pair,)), dma((n_pair,)), dma, dma,
            dma((octs, PARTS, n_group)), dma((octs, PARTS, n_group)), dma((PARTS,)), dma((PARTS,)),
        ],
        compiler_params=pltpu.CompilerParams(
            collective_id=0, has_side_effects=True, vmem_limit_bytes=48 * 1024 * 1024
        ),
        name="cycle",
    )(
        swapped, cell_class, land_mask, kappa, flow,
        obs_index.reshape(1, n_obs), obs_values.reshape(1, n_obs), obs_var.reshape(1, n_obs),
    )
    return out.transpose(1, 0, 2)


def solution(mesh):
    return jax.shard_map(
        functools.partial(local, mesh.shape["slab"], mesh.shape["mem"]),
        mesh=mesh,
        in_specs=(
            P("mem", "slab", None),
            P("slab", None),
            P("slab", None),
            P(),
            P(),
            P("slab"),
            P("slab"),
            P("slab"),
        ),
        out_specs=P("mem", "slab", None),
        check_vma=False,
    )
```

```python
import functools

import jax
import jax.numpy as jnp
from jax import lax
from jax.experimental import pallas as pl
from jax.experimental.pallas import tpu as pltpu
from jax.sharding import PartitionSpec as P

STEPS = 8
ROOT_ITERATIONS = 8
NCLS = 8
HEIGHT = 4
SPLIT = 4
PARTS = 2


def halves(x):
    high = x.astype(jnp.bfloat16)
    return high, (x - high.astype(jnp.float32)).astype(jnp.bfloat16)


def left_parts(x):
    high, low = halves(x)
    return jnp.concatenate([high, high, low], axis=1)


def right_parts(x):
    high, low = halves(x)
    return jnp.concatenate([high, low, high], axis=0)


def product(left, right):
    return jnp.dot(left, right, preferred_element_type=jnp.float32)


def dot(a, b):
    return product(left_parts(a), right_parts(b))


def cycle_kernel(
    n_slab, n_mem,
    states_in, classes_in, mask_in, kappa_in, flow_in, obs_index, obs_values, obs_var,
    out,
    raw, states, kappa, flow, load_sem, table_sem, own_sem, buf, coef, geos, gobs, gval, pick, hxs, gpart, precv, gfull, turned, fore, mixed,
    geo_send, geo_recv, obs_send, obs_recv, y_send, y_recv, d_send, d_recv, r_send, r_recv, keep_sem,
    h_send, h_recv, p_send, p_recv, g_send, g_recv, a_send, a_recv, b_send, b_recv,
):
    s = lax.axis_index("slab")
    m = lax.axis_index("mem")
    q, y = lax.div(s, 2), lax.rem(s, 2)
    n_pair, n_group = n_slab // 2, 2 * n_mem
    octs, rows, lon = states.shape[0], states.shape[1], states.shape[3]
    half = lon // 2
    ens = fore.shape[1]
    n_obs = gobs.shape[2]
    line, core = lax.div(m, 2), lax.rem(m, 2)
    sibling = 2 * line + 1 - core
    kd = octs * 16
    group = y * n_mem + m
    last = n_pair - 1
    step_pair = 2 * y - 1

    def device(pair, side, member):
        return (2 * pair + side, member)

    def remote(src, dst, send, recv, where):
        return pltpu.make_async_remote_copy(
            src_ref=src, dst_ref=dst, send_sem=send, recv_sem=recv,
            device_id=where, device_id_type=pl.DeviceIdType.MESH,
        )

    def peer(k):
        other = lax.rem(group + k, n_group)
        return other, lax.div(other, n_mem), lax.rem(other, n_mem)

    def load(side, c):
        which = octs * side + c
        return pltpu.make_async_copy(
            states_in.at[pl.ds(pl.multiple_of(8 * which, 8), 8)], raw.at[which], load_sem.at[which]
        )

    own_loads = [
        pltpu.make_async_copy(classes_in, geos.at[1 + y, 0], own_sem.at[0]),
        pltpu.make_async_copy(mask_in, geos.at[1 + y, 1], own_sem.at[1]),
        pltpu.make_async_copy(obs_index, gobs.at[y], own_sem.at[2]),
        pltpu.make_async_copy(obs_values, gval.at[y, 0], own_sem.at[3]),
        pltpu.make_async_copy(obs_var, gval.at[y, 1], own_sem.at[4]),
    ]
    table_loads = [
        pltpu.make_async_copy(kappa_in, kappa, table_sem.at[0]),
        pltpu.make_async_copy(flow_in, flow, table_sem.at[1]),
    ]

    barrier = pltpu.get_barrier_semaphore()
    for k in range(1, n_group):
        _, ty, tm = peer(k)
        pl.semaphore_signal(barrier, inc=1, device_id=device(q, ty, tm), device_id_type=pl.DeviceIdType.MESH)
    for k in range(1, n_pair):
        tq = lax.rem(q + k, n_pair)
        pl.semaphore_signal(barrier, inc=1, device_id=device(tq, y, m), device_id_type=pl.DeviceIdType.MESH)
    for c in range(octs):
        load(1 - y, c).start()
    for c in range(octs):
        load(y, c).start()
    for copy in own_loads + table_loads:
        copy.start()
    for c in range(octs):
        load(1 - y, c).wait()
        states[c] = jnp.swapaxes(raw[octs * (1 - y) + c], 0, 1)
    for c in range(octs):
        load(y, c).wait()
        buf[0, c, pl.ds(8 + 8 * y, 8)] = jnp.swapaxes(raw[octs * y + c], 0, 1)
    for copy in own_loads + table_loads:
        copy.wait()
    pl.semaphore_wait(barrier, n_group - 1 + n_pair - 1)

    piece = 8 // SPLIT

    def y_copy(c, h):
        return remote(
            states.at[c, pl.ds(piece * h, piece)], buf.at[0, c, pl.ds(8 + 8 * y + piece * h, piece)],
            y_send.at[c, h], y_recv.at[c, h], device(q, 1 - y, m),
        )

    def y_wait(c, h):
        return remote(
            states.at[c, pl.ds(0, piece)], buf.at[0, c, pl.ds(16 - 8 * y + piece * h, piece)],
            y_send.at[c, h], y_recv.at[c, h], device(q, 1 - y, m),
        )

    def direct_copy(c):
        return remote(
            buf.at[0, c, pl.ds(8 + 8 * y, 8)], buf.at[0, c, pl.ds(24 * (1 - y), 8)],
            d_send.at[c], d_recv.at[c], device(q + step_pair, y, m),
        )

    def relay_copy(c, h):
        return remote(
            buf.at[0, c, pl.ds(16 - 8 * y + piece * h, piece)], buf.at[0, c, pl.ds(24 * y + piece * h, piece)],
            r_send.at[c, h], r_recv.at[c, h], device(q - step_pair, y, m),
        )

    fields = (geos.at[1 + y, 0], geos.at[1 + y, 1])

    def geo_pair(f):
        return remote(
            fields[f], geos.at[1 + y, f], geo_send.at[0, f], geo_recv.at[1 + y, f], device(q, 1 - y, m)
        )

    def geo_direct(f):
        return remote(
            fields[f], geos.at[3 * (1 - y), f], geo_send.at[1, f], geo_recv.at[3 * (1 - y), f],
            device(q + step_pair, y, m),
        )

    def geo_relay(f):
        return remote(
            geos.at[2 - y, f], geos.at[3 * y, f], geo_send.at[2, f], geo_recv.at[3 * y, f],
            device(q - step_pair, y, m),
        )

    def geo_wait(slot, f):
        return remote(fields[f], geos.at[slot, f], geo_send.at[0, f], geo_recv.at[slot, f], device(q, 1 - y, m))

    observed = (gobs.at[y], gval.at[y, 0], gval.at[y, 1])
    other_observed = (gobs.at[1 - y], gval.at[1 - y, 0], gval.at[1 - y, 1])

    def obs_copy(f):
        return remote(observed[f], observed[f], obs_send.at[f], obs_recv.at[f], device(q, 1 - y, m))

    def obs_wait(f):
        return remote(other_observed[f], other_observed[f], obs_send.at[f], obs_recv.at[f], device(q, 1 - y, m))

    forward_edge = (q + step_pair >= 0) & (q + step_pair <= last)
    backward_edge = (q - step_pair >= 0) & (q - step_pair <= last)

    for f in range(2):
        geo_pair(f).start()
    for f in range(3):
        obs_copy(f).start()
    for c in range(octs):
        for h in range(SPLIT):
            y_copy(c, h).start()

    @pl.when(forward_edge)
    def _():
        for f in range(2):
            geo_direct(f).start()
        for c in range(octs):
            direct_copy(c).start()

    @pl.when(q == 0)
    def _():
        geos[0] = jnp.zeros(geos.shape[1:], jnp.int32)
        for c in range(octs):
            buf[0, c, 0:8] = jnp.zeros((8, 8, lon), jnp.float32)

    @pl.when(q == last)
    def _():
        geos[3] = jnp.zeros(geos.shape[1:], jnp.int32)
        for c in range(octs):
            buf[0, c, 24:32] = jnp.zeros((8, 8, lon), jnp.float32)

    for f in range(2):
        geo_wait(2 - y, f).wait_recv()

    @pl.when(backward_edge)
    def _():
        for f in range(2):
            geo_relay(f).start()
            geo_wait(3 * (1 - y), f).wait_recv()

    lane = lax.broadcasted_iota(jnp.int32, (8, lon), 1)

    def coefficients(k, carry):
        classes = geos[k, 0]
        wet = geos[k, 1].astype(jnp.float32)
        diffusion = jnp.zeros(classes.shape, jnp.float32)
        east = jnp.zeros(classes.shape, jnp.float32)
        north = jnp.zeros(classes.shape, jnp.float32)
        for label in range(NCLS):
            hit = classes == label
            diffusion = jnp.where(hit, kappa[label], diffusion)
            east = jnp.where(hit, flow[0, label], east)
            north = jnp.where(hit, flow[1, label], north)
        terms = (
            wet * (1.0 - 4.0 * diffusion),
            wet * (diffusion - 0.5 * north),
            wet * (diffusion + 0.5 * north),
            jnp.where(lane == lon - 1, 0.0, wet * (diffusion - 0.5 * east)),
            jnp.where(lane == 0, 0.0, wet * (diffusion + 0.5 * east)),
        )
        for index, term in enumerate(terms):
            for row in range(8):
                coef[8 * k + row, index] = jnp.broadcast_to(term[row : row + 1], (8, lon))
        return carry

    lax.fori_loop(1 - y, 4 - y, coefficients, 0)

    for f in range(3):
        obs_wait(f).wait_recv()
    place = jnp.concatenate([gobs[0], gobs[1]], axis=1)
    column = place & (lon - 1)
    pick[...] = jnp.where(
        lax.broadcasted_iota(jnp.int32, (lon, 2 * n_obs), 0) == column, 1.0, 0.0
    ).astype(jnp.bfloat16)
    side = lax.div(lax.broadcasted_iota(jnp.int32, (1, 2 * n_obs), 1), n_obs)
    obs_row = rows * side + (place >> (lon.bit_length() - 1))

    @pl.when(forward_edge)
    def _():
        for f in range(2):
            geo_wait(3 * y, f).wait_recv()

    lax.fori_loop(3 * y, 3 * y + 1, coefficients, 0)

    def relay(c, h):
        y_wait(c, h).wait_recv()

        @pl.when(backward_edge)
        def _():
            relay_copy(c, h).start()

    def advance(c, source, target, height, base):
        level = [buf[source, c, base - 1 + k] for k in range(height + 2)]
        fresh = []
        for k in range(height):
            center = level[k + 1]
            fresh.append(
                coef[base + k, 0] * center
                + coef[base + k, 1] * level[k + 2]
                + coef[base + k, 2] * level[k]
                + coef[base + k, 3] * pltpu.roll(center, lon - 1, 1)
                + coef[base + k, 4] * pltpu.roll(center, 1, 1)
            )
        for k in range(height):
            buf[target, c, base + k] = fresh[k]

    def buffers(pair_step, parity):
        if parity == 0:
            return jnp.where(pair_step == 0, 0, 2), 1
        return 1, 2

    def early(c):
        def two_steps(pair_step, carry):
            for parity in range(2):
                step = 2 * pair_step + parity + 1
                source, target = buffers(pair_step, parity)
                first = step + 8 * (1 - y)
                full = lax.div(24 - 2 * step, HEIGHT)

                def some(g, inner):
                    advance(c, source, target, HEIGHT, first + HEIGHT * g)
                    return inner

                lax.fori_loop(0, full, some, 0)
                if parity == 0:
                    advance(c, source, target, 2, first + 22 - 2 * step)
            return carry

        lax.fori_loop(0, STEPS // 2, two_steps, 0)

    def late(c):
        def two_steps(pair_step, carry):
            for parity in range(2):
                step = 2 * pair_step + parity + 1
                source, target = buffers(pair_step, parity)
                first = step + y * (24 - 2 * step)

                def some(g, inner):
                    advance(c, source, target, HEIGHT, first + HEIGHT * g)
                    return inner

                lax.fori_loop(0, 8 // HEIGHT, some, 0)
            return carry

        lax.fori_loop(0, STEPS // 2, two_steps, 0)

    def direct_arrived(c):
        @pl.when(backward_edge)
        def _():
            remote(states.at[c], buf.at[0, c, pl.ds(24 * (1 - y), 8)], d_send.at[c], d_recv.at[c], device(q, 1 - y, m)).wait_recv()

    def relay_arrived(c):
        @pl.when(forward_edge)
        def _():
            for h in range(SPLIT):
                remote(
                    states.at[c, pl.ds(0, piece)], buf.at[0, c, pl.ds(24 * y + piece * h, piece)],
                    r_send.at[c, h], r_recv.at[c, h], device(q, 1 - y, m),
                ).wait_recv()

    deep = rows // PARTS

    def a_copy(c, h, other, ty, tm):
        return remote(
            buf.at[2, c, pl.ds(8 + 8 * ty + deep * h, deep), :, pl.ds(pl.multiple_of(half * lax.rem(tm, 2), 128), half)],
            fore.at[pl.ds(deep * h, deep), pl.ds(pl.multiple_of(kd * m + 8 * octs * y + 8 * c, 8), 8), :],
            a_send.at[c, h, other], a_recv.at[c, h, group], device(q, ty, tm),
        )

    def a_wait(c, h, other, ty, tm):
        return remote(
            buf.at[2, c, pl.ds(8, deep), :, pl.ds(0, half)],
            fore.at[pl.ds(deep * h, deep), pl.ds(pl.multiple_of(kd * tm + 8 * octs * ty + 8 * c, 8), 8), :],
            a_send.at[c, h, other], a_recv.at[c, h, other], device(q, ty, tm),
        )

    def a_keep(c, h):
        return pltpu.make_async_copy(
            buf.at[2, c, pl.ds(8 + 8 * y + deep * h, deep), :, pl.ds(pl.multiple_of(half * core, 128), half)],
            fore.at[pl.ds(deep * h, deep), pl.ds(pl.multiple_of(kd * m + 8 * octs * y + 8 * c, 8), 8), :],
            a_send.at[c, h, group],
        )

    def far_start(c, h):
        for k in range(n_mem):
            tm = lax.rem(m + 2 + k, n_mem)
            a_copy(c, h, (1 - y) * n_mem + tm, 1 - y, tm).start()

    def near_start(c, h):
        for k in range(1, n_mem):
            tm = lax.rem(m + k, n_mem)
            a_copy(c, h, y * n_mem + tm, y, tm).start()
        a_keep(c, h).start()

    own_rows = kd * m + 8 * octs * y

    def observe(c):
        rest = buf[2, c, 8:24].reshape(16 * 8, lon)
        pieces = []
        for _ in range(3):
            part = rest.astype(jnp.bfloat16)
            pieces.append(part)
            rest = rest - part.astype(jnp.float32)
        seen = jnp.dot(jnp.concatenate(pieces, axis=0), pick[...], preferred_element_type=jnp.float32)
        seen = seen[:128] + seen[128:256] + seen[256:]
        hx = jnp.zeros((8, 2 * n_obs), jnp.float32)
        for row in range(2 * rows):
            hx = hx + jnp.where(obs_row == row, seen[8 * row : 8 * row + 8], 0.0)
        hxs[pl.ds(pl.multiple_of(own_rows + 8 * c, 8), 8)] = hx

    for h in range(SPLIT):
        relay(0, h)
    direct_arrived(0)
    early(0)
    far_start(0, 0)
    for c in range(octs):
        if c < octs - 1:
            for h in range(SPLIT // 2):
                relay(c + 1, h)
        relay_arrived(c)
        late(c)
        if c < octs - 1:
            for h in range(PARTS):
                near_start(c, h)
            for h in range(SPLIT // 2, SPLIT):
                relay(c + 1, h)
            direct_arrived(c + 1)
            early(c + 1)
            observe(c)
    observe(octs - 1)

    mine = pl.ds(pl.multiple_of(own_rows, 8), 8 * octs)

    def h_copy(other, ty, tm):
        return remote(hxs.at[mine], hxs.at[mine], h_send.at[other], h_recv.at[group], device(q, ty, tm))

    def h_wait(other, ty, tm):
        there = hxs.at[pl.ds(pl.multiple_of(kd * tm + 8 * octs * ty, 8), 8 * octs)]
        return remote(there, there, h_send.at[other], h_recv.at[other], device(q, ty, tm))

    for k in range(1, n_group):
        h_copy(*peer(k)).start()
    for h in range(PARTS):
        for c in range(octs):
            if h > 0 or c > 0:
                far_start(c, h)
        for c in range(1, octs):
            near_start(c, h)
    for k in range(1, n_group):
        h_wait(*peer(k)).wait_recv()

    share = ens // 2
    full = hxs[...]
    ybar = jnp.sum(full, axis=0, keepdims=True) / ens
    slab = (2 * q + side).astype(jnp.float32)
    err = jnp.concatenate([gval[0, 1], gval[1, 1]], axis=1) * (1.0 + 2.0 * slab / float(n_slab - 1))
    scaled = jnp.sqrt(err * (ens - 1.0))
    anom = (full - ybar) / scaled
    part = (hxs[pl.ds(pl.multiple_of(share * core, 8), share)] - ybar) / scaled
    dev = (jnp.concatenate([gval[0, 0], gval[1, 0]], axis=1) - ybar) / jnp.sqrt(err)
    both = jnp.concatenate([part, jnp.broadcast_to(dev, (16, 2 * n_obs))], axis=0)
    high, low = halves(anom)
    sums = lax.dot_general(
        left_parts(both), jnp.concatenate([high, low, high], axis=1), (((1,), (1,)), ((), ())),
        preferred_element_type=jnp.float32,
    )
    gpart[...] = sums[: share + 8]

    def p_copy(k):
        tq = lax.rem(q + k, n_pair)
        return remote(gpart, precv.at[q], p_send.at[tq], p_recv.at[q], device(tq, y, m))

    def p_wait(k):
        tq = lax.rem(q + k, n_pair)
        return remote(gpart, precv.at[tq], p_send.at[tq], p_recv.at[tq], device(tq, y, m))

    for k in range(1, n_pair):
        p_copy(k).start()
    precv[q] = sums[: share + 8]
    for k in range(1, n_pair):
        p_wait(k).wait_recv()
    total = precv[0]
    for k in range(1, n_pair):
        total = total + precv[k]
    own = pl.ds(pl.multiple_of(share * core, 8), share)
    theirs = pl.ds(pl.multiple_of(share * (1 - core), 8), share)
    gfull[own] = total[:share]
    g_copy = remote(gfull.at[own], gfull.at[own], g_send, g_recv, device(q, y, sibling))
    g_copy.start()
    proj = jnp.concatenate([total[share:], total[share:]], axis=0)
    remote(gfull.at[theirs], gfull.at[theirs], g_send, g_recv, device(q, y, sibling)).wait_recv()

    ident = jnp.where(
        lax.broadcasted_iota(jnp.int32, (ens, ens), 0) == lax.broadcasted_iota(jnp.int32, (ens, ens), 1), 1.0, 0.0
    )
    matrix = ident + gfull[...]
    scale = jnp.sum(jnp.sum(matrix * ident, axis=1, keepdims=True), axis=0, keepdims=True)

    upper = matrix / scale
    factor = 1.5 * ident - 0.5 * upper
    upper, lower = dot(upper, factor), factor
    for turn in range(ROOT_ITERATIONS - 1):
        factor = 1.5 * ident - 0.5 * dot(lower, upper)
        if turn < ROOT_ITERATIONS - 2:
            upper = dot(upper, factor)
        lower = dot(factor, lower)
    high, low = halves(proj)
    once = lax.dot_general(
        left_parts(lower), jnp.concatenate([high, low, high], axis=1), (((1,), (1,)), ((), ())),
        preferred_element_type=jnp.float32,
    )
    mean_w = dot(lower, once)[:, :1] / (scale * jnp.sqrt(jnp.float32(ens - 1.0)))
    total_w = lower / jnp.sqrt(scale) + mean_w
    omega = 1.0 / ens + total_w - jnp.sum(total_w, axis=0, keepdims=True) / ens
    turned[...] = omega.T
    weights = left_parts(
        jnp.concatenate(
            [turned[pl.ds(pl.multiple_of(kd * m, 8), kd)], turned[pl.ds(pl.multiple_of(kd * sibling, 8), kd)]], axis=0
        )
    )

    def b_copy(h):
        return remote(
            mixed.at[pl.ds(deep * h, deep)],
            out.at[pl.ds(deep * h, deep), :, pl.ds(pl.multiple_of(half * core, 128), half)],
            b_send.at[h], b_recv.at[h], device(q, y, sibling),
        )

    def b_wait(h):
        return remote(
            mixed.at[pl.ds(deep * h, deep)],
            out.at[pl.ds(deep * h, deep), :, pl.ds(pl.multiple_of(half * (1 - core), 128), half)],
            b_send.at[h], b_recv.at[h], device(q, y, sibling),
        )

    for h in range(PARTS):
        for c in range(octs):
            a_keep(c, h).wait()
            for k in range(1, n_group):
                a_wait(c, h, *peer(k)).wait_recv()
        for row in range(deep * h, deep * h + deep):
            result = product(weights, right_parts(fore[row]))
            mixed[row] = result[kd:]
            out[row, :, pl.ds(pl.multiple_of(half * core, 128), half)] = result[:kd]
        b_copy(h).start()

    for f in range(2):
        geo_pair(f).wait_send()
    for f in range(3):
        obs_copy(f).wait_send()
    for c in range(octs):
        for h in range(SPLIT):
            y_copy(c, h).wait_send()

    @pl.when(forward_edge)
    def _():
        for f in range(2):
            geo_direct(f).wait_send()
        for c in range(octs):
            direct_copy(c).wait_send()

    @pl.when(backward_edge)
    def _():
        for f in range(2):
            geo_relay(f).wait_send()
        for c in range(octs):
            for h in range(SPLIT):
                relay_copy(c, h).wait_send()

    for k in range(1, n_group):
        for c in range(octs):
            for h in range(PARTS):
                a_copy(c, h, *peer(k)).wait_send()
        h_copy(*peer(k)).wait_send()
    for k in range(1, n_pair):
        p_copy(k).wait_send()
    g_copy.wait_send()
    for h in range(PARTS):
        b_copy(h).wait_send()
        b_wait(h).wait_recv()


def local(n_slab, n_mem, states, land_mask, cell_class, kappa, flow, obs_index, obs_values, obs_var):
    kd, rows, lon = states.shape
    ens = kd * n_mem
    n_pair, n_group, octs = n_slab // 2, 2 * n_mem, kd // 16
    n_obs = obs_index.shape[0]
    dma = pltpu.SemaphoreType.DMA
    vmem = pl.BlockSpec(memory_space=pltpu.VMEM)
    hbm = pl.BlockSpec(memory_space=pltpu.HBM)
    f32 = jnp.float32
    out = pl.pallas_call(
        functools.partial(cycle_kernel, n_slab, n_mem),
        out_shape=jax.ShapeDtypeStruct((rows, kd, lon), f32),
        in_specs=[hbm] * 8,
        out_specs=vmem,
        scratch_shapes=[
            pltpu.VMEM((2 * octs, 8, rows, lon), f32),
            pltpu.VMEM((octs, rows, 8, lon), f32),
            pltpu.SMEM(kappa.shape, f32),
            pltpu.SMEM(flow.shape, f32),
            dma((2 * octs,)), dma((2,)), dma((5,)),
            pltpu.VMEM((3, octs, 4 * rows, 8, lon), f32),
            pltpu.VMEM((4 * rows, 5, 8, lon), f32),
            pltpu.VMEM((4, 2, rows, lon), jnp.int32),
            pltpu.VMEM((2, 1, n_obs), jnp.int32),
            pltpu.VMEM((2, 2, 1, n_obs), f32),
            pltpu.VMEM((lon, 2 * n_obs), jnp.bfloat16),
            pltpu.VMEM((ens, 2 * n_obs), f32),
            pltpu.VMEM((ens // 2 + 8, ens), f32),
            pltpu.VMEM((n_pair, ens // 2 + 8, ens), f32),
            pltpu.VMEM((ens, ens), f32),
            pltpu.VMEM((ens, ens), f32),
            pltpu.VMEM((rows, ens, lon // 2), f32),
            pltpu.VMEM((rows, kd, lon // 2), f32),
            dma((3, 2)), dma((4, 2)), dma((3,)), dma((3,)), dma((octs, SPLIT)), dma((octs, SPLIT)),
            dma((octs,)), dma((octs,)), dma((octs, SPLIT)), dma((octs, SPLIT)), dma((octs,)),
            dma((n_group,)), dma((n_group,)), dma((n_pair,)), dma((n_pair,)), dma, dma,
            dma((octs, PARTS, n_group)), dma((octs, PARTS, n_group)), dma((PARTS,)), dma((PARTS,)),
        ],
        compiler_params=pltpu.CompilerParams(
            collective_id=0, has_side_effects=True, vmem_limit_bytes=48 * 1024 * 1024
        ),
        name="cycle",
    )(
        *(
            pltpu.with_memory_space_constraint(array, pltpu.HBM)
            for array in (
                states, cell_class, land_mask, kappa, flow,
                obs_index.reshape(1, n_obs), obs_values.reshape(1, n_obs), obs_var.reshape(1, n_obs),
            )
        )
    )
    return out.transpose(1, 0, 2)


def solution(mesh):
    return jax.shard_map(
        functools.partial(local, mesh.shape["slab"], mesh.shape["mem"]),
        mesh=mesh,
        in_specs=(
            P("mem", "slab", None),
            P("slab", None),
            P("slab", None),
            P(),
            P(),
            P("slab"),
            P("slab"),
            P("slab"),
        ),
        out_specs=P("mem", "slab", None),
        check_vma=False,
    )
```

```python
import functools

import jax
import jax.numpy as jnp
from jax import lax
from jax.experimental import pallas as pl
from jax.experimental.pallas import tpu as pltpu
from jax.sharding import PartitionSpec as P

STEPS = 8
ROOT_ITERATIONS = 8
NCLS = 8
HEIGHT = 8
SPLIT = 4
PARTS = 2


def halves(x):
    high = x.astype(jnp.bfloat16)
    return high, (x - high.astype(jnp.float32)).astype(jnp.bfloat16)


def left_parts(x):
    high, low = halves(x)
    return jnp.concatenate([high, high, low], axis=1)


def right_parts(x):
    high, low = halves(x)
    return jnp.concatenate([high, low, high], axis=0)


def product(left, right):
    return jnp.dot(left, right, preferred_element_type=jnp.float32)


def dot(a, b):
    return product(left_parts(a), right_parts(b))


def cycle_kernel(
    n_slab, n_mem,
    states_in, classes_in, mask_in, kappa_in, flow_in, obs_index, obs_values, obs_var,
    out,
    raw, states, kappa, flow, load_sem, table_sem, own_sem, land, odd, even, coef, geos, gobs, gval, pick, hxs, gpart, precv, gfull, turned, fore, mixed,
    geo_send, geo_recv, obs_send, obs_recv, y_send, y_recv, d_send, d_recv, r_send, r_recv, keep_sem,
    h_send, h_recv, p_send, p_recv, g_send, g_recv, a_send, a_recv, b_send, b_recv,
):
    s = lax.axis_index("slab")
    m = lax.axis_index("mem")
    q, y = lax.div(s, 2), lax.rem(s, 2)
    n_pair, n_group = n_slab // 2, 2 * n_mem
    octs, rows, lon = states.shape[0], states.shape[1], states.shape[3]
    half = lon // 2
    ens = fore.shape[1]
    n_obs = gobs.shape[2]
    line, core = lax.div(m, 2), lax.rem(m, 2)
    sibling = 2 * line + 1 - core
    kd = octs * 16
    group = y * n_mem + m
    last = n_pair - 1
    step_pair = 2 * y - 1

    def device(pair, side, member):
        return (2 * pair + side, member)

    def remote(src, dst, send, recv, where):
        return pltpu.make_async_remote_copy(
            src_ref=src, dst_ref=dst, send_sem=send, recv_sem=recv,
            device_id=where, device_id_type=pl.DeviceIdType.MESH,
        )

    def peer(k):
        other = lax.rem(group + k, n_group)
        return other, lax.div(other, n_mem), lax.rem(other, n_mem)

    def load(side, c):
        which = octs * side + c
        return pltpu.make_async_copy(
            states_in.at[pl.ds(pl.multiple_of(8 * which, 8), 8)], raw.at[which], load_sem.at[which]
        )

    own_loads = [
        pltpu.make_async_copy(classes_in, geos.at[1 + y, 0], own_sem.at[0]),
        pltpu.make_async_copy(mask_in, geos.at[1 + y, 1], own_sem.at[1]),
        pltpu.make_async_copy(obs_index, gobs.at[y], own_sem.at[2]),
        pltpu.make_async_copy(obs_values, gval.at[y, 0], own_sem.at[3]),
        pltpu.make_async_copy(obs_var, gval.at[y, 1], own_sem.at[4]),
    ]
    table_loads = [
        pltpu.make_async_copy(kappa_in, kappa, table_sem.at[0]),
        pltpu.make_async_copy(flow_in, flow, table_sem.at[1]),
    ]

    barrier = pltpu.get_barrier_semaphore()
    for k in range(1, n_group):
        _, ty, tm = peer(k)
        pl.semaphore_signal(barrier, inc=1, device_id=device(q, ty, tm), device_id_type=pl.DeviceIdType.MESH)
    for k in range(1, n_pair):
        tq = lax.rem(q + k, n_pair)
        pl.semaphore_signal(barrier, inc=1, device_id=device(tq, y, m), device_id_type=pl.DeviceIdType.MESH)
    for c in range(octs):
        load(1 - y, c).start()
    for c in range(octs):
        load(y, c).start()
    for copy in own_loads + table_loads:
        copy.start()
    for c in range(octs):
        load(1 - y, c).wait()
        states[c] = jnp.swapaxes(raw[octs * (1 - y) + c], 0, 1)
    for c in range(octs):
        load(y, c).wait()
        land[c, pl.ds(8 + 8 * y, 8)] = jnp.swapaxes(raw[octs * y + c], 0, 1)
    for copy in own_loads + table_loads:
        copy.wait()
    pl.semaphore_wait(barrier, n_group - 1 + n_pair - 1)

    piece = 8 // SPLIT

    def y_copy(c, h):
        return remote(
            states.at[c, pl.ds(piece * h, piece)], land.at[c, pl.ds(8 + 8 * y + piece * h, piece)],
            y_send.at[c, h], y_recv.at[c, h], device(q, 1 - y, m),
        )

    def y_wait(c, h):
        return remote(
            states.at[c, pl.ds(0, piece)], land.at[c, pl.ds(16 - 8 * y + piece * h, piece)],
            y_send.at[c, h], y_recv.at[c, h], device(q, 1 - y, m),
        )

    def direct_copy(c):
        return remote(
            land.at[c, pl.ds(8 + 8 * y, 8)], land.at[c, pl.ds(24 * (1 - y), 8)],
            d_send.at[c], d_recv.at[c], device(q + step_pair, y, m),
        )

    def relay_copy(c, h):
        return remote(
            land.at[c, pl.ds(16 - 8 * y + piece * h, piece)], land.at[c, pl.ds(24 * y + piece * h, piece)],
            r_send.at[c, h], r_recv.at[c, h], device(q - step_pair, y, m),
        )

    fields = (geos.at[1 + y, 0], geos.at[1 + y, 1])

    def geo_pair(f):
        return remote(
            fields[f], geos.at[1 + y, f], geo_send.at[0, f], geo_recv.at[1 + y, f], device(q, 1 - y, m)
        )

    def geo_direct(f):
        return remote(
            fields[f], geos.at[3 * (1 - y), f], geo_send.at[1, f], geo_recv.at[3 * (1 - y), f],
            device(q + step_pair, y, m),
        )

    def geo_relay(f):
        return remote(
            geos.at[2 - y, f], geos.at[3 * y, f], geo_send.at[2, f], geo_recv.at[3 * y, f],
            device(q - step_pair, y, m),
        )

    def geo_wait(slot, f):
        return remote(fields[f], geos.at[slot, f], geo_send.at[0, f], geo_recv.at[slot, f], device(q, 1 - y, m))

    observed = (gobs.at[y], gval.at[y, 0], gval.at[y, 1])
    other_observed = (gobs.at[1 - y], gval.at[1 - y, 0], gval.at[1 - y, 1])

    def obs_copy(f):
        return remote(observed[f], observed[f], obs_send.at[f], obs_recv.at[f], device(q, 1 - y, m))

    def obs_wait(f):
        return remote(other_observed[f], other_observed[f], obs_send.at[f], obs_recv.at[f], device(q, 1 - y, m))

    forward_edge = (q + step_pair >= 0) & (q + step_pair <= last)
    backward_edge = (q - step_pair >= 0) & (q - step_pair <= last)

    for f in range(2):
        geo_pair(f).start()
    for f in range(3):
        obs_copy(f).start()
    for c in range(octs):
        for h in range(SPLIT):
            y_copy(c, h).start()

    @pl.when(forward_edge)
    def _():
        for f in range(2):
            geo_direct(f).start()
        for c in range(octs):
            direct_copy(c).start()

    @pl.when(q == 0)
    def _():
        geos[0] = jnp.zeros(geos.shape[1:], jnp.int32)
        for c in range(octs):
            land[c, 0:8] = jnp.zeros((8, 8, lon), jnp.float32)

    @pl.when(q == last)
    def _():
        geos[3] = jnp.zeros(geos.shape[1:], jnp.int32)
        for c in range(octs):
            land[c, 24:32] = jnp.zeros((8, 8, lon), jnp.float32)

    for f in range(2):
        geo_wait(2 - y, f).wait_recv()

    @pl.when(backward_edge)
    def _():
        for f in range(2):
            geo_relay(f).start()
            geo_wait(3 * (1 - y), f).wait_recv()

    lane = lax.broadcasted_iota(jnp.int32, (8, lon), 1)

    def coefficients(k, carry):
        classes = geos[k, 0]
        wet = geos[k, 1].astype(jnp.float32)
        diffusion = jnp.zeros(classes.shape, jnp.float32)
        east = jnp.zeros(classes.shape, jnp.float32)
        north = jnp.zeros(classes.shape, jnp.float32)
        for label in range(NCLS):
            hit = classes == label
            diffusion = jnp.where(hit, kappa[label], diffusion)
            east = jnp.where(hit, flow[0, label], east)
            north = jnp.where(hit, flow[1, label], north)
        terms = (
            wet * (1.0 - 4.0 * diffusion),
            wet * (diffusion - 0.5 * north),
            wet * (diffusion + 0.5 * north),
            jnp.where(lane == lon - 1, 0.0, wet * (diffusion - 0.5 * east)),
            jnp.where(lane == 0, 0.0, wet * (diffusion + 0.5 * east)),
        )
        for index, term in enumerate(terms):
            for row in range(8):
                coef[8 * k + row, index] = jnp.broadcast_to(term[row : row + 1], (8, lon))
        return carry

    lax.fori_loop(1 - y, 4 - y, coefficients, 0)

    for f in range(3):
        obs_wait(f).wait_recv()
    place = jnp.concatenate([gobs[0], gobs[1]], axis=1)
    column = place & (lon - 1)
    pick[...] = jnp.where(
        lax.broadcasted_iota(jnp.int32, (lon, 2 * n_obs), 0) == column, 1.0, 0.0
    ).astype(jnp.bfloat16)
    side = lax.div(lax.broadcasted_iota(jnp.int32, (1, 2 * n_obs), 1), n_obs)
    obs_row = rows * side + (place >> (lon.bit_length() - 1))

    @pl.when(forward_edge)
    def _():
        for f in range(2):
            geo_wait(3 * y, f).wait_recv()

    lax.fori_loop(3 * y, 3 * y + 1, coefficients, 0)

    def relay(c, h):
        y_wait(c, h).wait_recv()

        @pl.when(backward_edge)
        def _():
            relay_copy(c, h).start()

    def advance(c, source, target, height, base):
        level = [source[c, base - 1], source[c, base]]
        for k in range(height):
            level.append(source[c, base + k + 1])
            south, center, north = level[k : k + 3]
            target[c, base + k] = (
                coef[base + k, 0] * center
                + coef[base + k, 1] * north
                + coef[base + k, 2] * south
                + coef[base + k, 3] * pltpu.roll(center, lon - 1, 1)
                + coef[base + k, 4] * pltpu.roll(center, 1, 1)
            )

    def rows_at(step, c, first, count):
        source = land if step == 1 else (odd, even)[step % 2]
        target = (even, odd)[step % 2]

        def some(g, inner):
            advance(c, source, target, HEIGHT, first + HEIGHT * g)
            return inner

        full = count // HEIGHT
        if full > 1:
            lax.fori_loop(0, full, some, 0)
        elif full == 1:
            some(0, 0)
        if count % HEIGHT:
            advance(c, source, target, count % HEIGHT, first + HEIGHT * full)

    def early(c):
        for step in range(1, STEPS + 1):
            rows_at(step, c, step + 8 * (1 - y), 24 - 2 * step)

    def late(c):
        for step in range(1, STEPS + 1):
            rows_at(step, c, step + y * (24 - 2 * step), 8)

    def direct_arrived(c):
        @pl.when(backward_edge)
        def _():
            remote(states.at[c], land.at[c, pl.ds(24 * (1 - y), 8)], d_send.at[c], d_recv.at[c], device(q, 1 - y, m)).wait_recv()

    def relay_arrived(c):
        @pl.when(forward_edge)
        def _():
            for h in range(SPLIT):
                remote(
                    states.at[c, pl.ds(0, piece)], land.at[c, pl.ds(24 * y + piece * h, piece)],
                    r_send.at[c, h], r_recv.at[c, h], device(q, 1 - y, m),
                ).wait_recv()

    deep = rows // PARTS

    def a_copy(c, h, other, ty, tm):
        return remote(
            even.at[c, pl.ds(8 + 8 * ty + deep * h, deep), :, pl.ds(pl.multiple_of(half * lax.rem(tm, 2), 128), half)],
            fore.at[pl.ds(deep * h, deep), pl.ds(pl.multiple_of(kd * m + 8 * octs * y + 8 * c, 8), 8), :],
            a_send.at[c, h, other], a_recv.at[c, h, group], device(q, ty, tm),
        )

    def a_wait(c, h, other, ty, tm):
        return remote(
            even.at[c, pl.ds(8, deep), :, pl.ds(0, half)],
            fore.at[pl.ds(deep * h, deep), pl.ds(pl.multiple_of(kd * tm + 8 * octs * ty + 8 * c, 8), 8), :],
            a_send.at[c, h, other], a_recv.at[c, h, other], device(q, ty, tm),
        )

    def a_keep(c, h):
        return pltpu.make_async_copy(
            even.at[c, pl.ds(8 + 8 * y + deep * h, deep), :, pl.ds(pl.multiple_of(half * core, 128), half)],
            fore.at[pl.ds(deep * h, deep), pl.ds(pl.multiple_of(kd * m + 8 * octs * y + 8 * c, 8), 8), :],
            a_send.at[c, h, group],
        )

    def far_start(c, h):
        for k in range(n_mem):
            tm = lax.rem(m + 2 + k, n_mem)
            a_copy(c, h, (1 - y) * n_mem + tm, 1 - y, tm).start()

    def near_start(c, h):
        for k in range(1, n_mem):
            tm = lax.rem(m + k, n_mem)
            a_copy(c, h, y * n_mem + tm, y, tm).start()
        a_keep(c, h).start()

    own_rows = kd * m + 8 * octs * y

    def observe(c):
        rest = even[c, 8:24].reshape(16 * 8, lon)
        pieces = []
        for _ in range(3):
            part = rest.astype(jnp.bfloat16)
            pieces.append(part)
            rest = rest - part.astype(jnp.float32)
        seen = jnp.dot(jnp.concatenate(pieces, axis=0), pick[...], preferred_element_type=jnp.float32)
        seen = seen[:128] + seen[128:256] + seen[256:]
        hx = jnp.zeros((8, 2 * n_obs), jnp.float32)
        for row in range(2 * rows):
            hx = hx + jnp.where(obs_row == row, seen[8 * row : 8 * row + 8], 0.0)
        hxs[pl.ds(pl.multiple_of(own_rows + 8 * c, 8), 8)] = hx

    for h in range(SPLIT):
        relay(0, h)
    direct_arrived(0)
    early(0)
    far_start(0, 0)
    for c in range(octs):
        if c < octs - 1:
            for h in range(SPLIT // 2):
                relay(c + 1, h)
        relay_arrived(c)
        late(c)
        if c < octs - 1:
            for h in range(PARTS):
                near_start(c, h)
            for h in range(SPLIT // 2, SPLIT):
                relay(c + 1, h)
            direct_arrived(c + 1)
            early(c + 1)
            observe(c)
    observe(octs - 1)

    mine = pl.ds(pl.multiple_of(own_rows, 8), 8 * octs)

    def h_copy(other, ty, tm):
        return remote(hxs.at[mine], hxs.at[mine], h_send.at[other], h_recv.at[group], device(q, ty, tm))

    def h_wait(other, ty, tm):
        there = hxs.at[pl.ds(pl.multiple_of(kd * tm + 8 * octs * ty, 8), 8 * octs)]
        return remote(there, there, h_send.at[other], h_recv.at[other], device(q, ty, tm))

    for k in range(1, n_group):
        h_copy(*peer(k)).start()
    for h in range(PARTS):
        for c in range(octs):
            if h > 0 or c > 0:
                far_start(c, h)
        for c in range(1, octs):
            near_start(c, h)
    for k in range(1, n_group):
        h_wait(*peer(k)).wait_recv()

    share = ens // 2
    full = hxs[...]
    ybar = jnp.sum(full, axis=0, keepdims=True) / ens
    slab = (2 * q + side).astype(jnp.float32)
    err = jnp.concatenate([gval[0, 1], gval[1, 1]], axis=1) * (1.0 + 2.0 * slab / float(n_slab - 1))
    scaled = jnp.sqrt(err * (ens - 1.0))
    anom = (full - ybar) / scaled
    part = (hxs[pl.ds(pl.multiple_of(share * core, 8), share)] - ybar) / scaled
    dev = (jnp.concatenate([gval[0, 0], gval[1, 0]], axis=1) - ybar) / jnp.sqrt(err)
    both = jnp.concatenate([part, jnp.broadcast_to(dev, (16, 2 * n_obs))], axis=0)
    high, low = halves(anom)
    sums = lax.dot_general(
        left_parts(both), jnp.concatenate([high, low, high], axis=1), (((1,), (1,)), ((), ())),
        preferred_element_type=jnp.float32,
    )
    gpart[...] = sums[: share + 8]

    def p_copy(k):
        tq = lax.rem(q + k, n_pair)
        return remote(gpart, precv.at[q], p_send.at[tq], p_recv.at[q], device(tq, y, m))

    def p_wait(k):
        tq = lax.rem(q + k, n_pair)
        return remote(gpart, precv.at[tq], p_send.at[tq], p_recv.at[tq], device(tq, y, m))

    for k in range(1, n_pair):
        p_copy(k).start()
    precv[q] = sums[: share + 8]
    for k in range(1, n_pair):
        p_wait(k).wait_recv()
    total = precv[0]
    for k in range(1, n_pair):
        total = total + precv[k]
    own = pl.ds(pl.multiple_of(share * core, 8), share)
    theirs = pl.ds(pl.multiple_of(share * (1 - core), 8), share)
    gfull[own] = total[:share]
    g_copy = remote(gfull.at[own], gfull.at[own], g_send, g_recv, device(q, y, sibling))
    g_copy.start()
    proj = jnp.concatenate([total[share:], total[share:]], axis=0)
    remote(gfull.at[theirs], gfull.at[theirs], g_send, g_recv, device(q, y, sibling)).wait_recv()

    ident = jnp.where(
        lax.broadcasted_iota(jnp.int32, (ens, ens), 0) == lax.broadcasted_iota(jnp.int32, (ens, ens), 1), 1.0, 0.0
    )
    matrix = ident + gfull[...]
    scale = jnp.sum(jnp.sum(matrix * ident, axis=1, keepdims=True), axis=0, keepdims=True)

    upper = matrix / scale
    factor = 1.5 * ident - 0.5 * upper
    upper, lower = dot(upper, factor), factor
    for turn in range(ROOT_ITERATIONS - 1):
        factor = 1.5 * ident - 0.5 * dot(lower, upper)
        if turn < ROOT_ITERATIONS - 2:
            upper = dot(upper, factor)
        lower = dot(factor, lower)
    high, low = halves(proj)
    once = lax.dot_general(
        left_parts(lower), jnp.concatenate([high, low, high], axis=1), (((1,), (1,)), ((), ())),
        preferred_element_type=jnp.float32,
    )
    mean_w = dot(lower, once)[:, :1] / (scale * jnp.sqrt(jnp.float32(ens - 1.0)))
    total_w = lower / jnp.sqrt(scale) + mean_w
    omega = 1.0 / ens + total_w - jnp.sum(total_w, axis=0, keepdims=True) / ens
    turned[...] = omega.T
    weights = left_parts(
        jnp.concatenate(
            [turned[pl.ds(pl.multiple_of(kd * m, 8), kd)], turned[pl.ds(pl.multiple_of(kd * sibling, 8), kd)]], axis=0
        )
    )

    def b_copy(h):
        return remote(
            mixed.at[pl.ds(deep * h, deep)],
            out.at[pl.ds(deep * h, deep), :, pl.ds(pl.multiple_of(half * core, 128), half)],
            b_send.at[h], b_recv.at[h], device(q, y, sibling),
        )

    def b_wait(h):
        return remote(
            mixed.at[pl.ds(deep * h, deep)],
            out.at[pl.ds(deep * h, deep), :, pl.ds(pl.multiple_of(half * (1 - core), 128), half)],
            b_send.at[h], b_recv.at[h], device(q, y, sibling),
        )

    for h in range(PARTS):
        for c in range(octs):
            a_keep(c, h).wait()
            for k in range(1, n_group):
                a_wait(c, h, *peer(k)).wait_recv()
        for row in range(deep * h, deep * h + deep):
            result = product(weights, right_parts(fore[row]))
            mixed[row] = result[kd:]
            out[row, :, pl.ds(pl.multiple_of(half * core, 128), half)] = result[:kd]
        b_copy(h).start()

    for f in range(2):
        geo_pair(f).wait_send()
    for f in range(3):
        obs_copy(f).wait_send()
    for c in range(octs):
        for h in range(SPLIT):
            y_copy(c, h).wait_send()

    @pl.when(forward_edge)
    def _():
        for f in range(2):
            geo_direct(f).wait_send()
        for c in range(octs):
            direct_copy(c).wait_send()

    @pl.when(backward_edge)
    def _():
        for f in range(2):
            geo_relay(f).wait_send()
        for c in range(octs):
            for h in range(SPLIT):
                relay_copy(c, h).wait_send()

    for k in range(1, n_group):
        for c in range(octs):
            for h in range(PARTS):
                a_copy(c, h, *peer(k)).wait_send()
        h_copy(*peer(k)).wait_send()
    for k in range(1, n_pair):
        p_copy(k).wait_send()
    g_copy.wait_send()
    for h in range(PARTS):
        b_copy(h).wait_send()
        b_wait(h).wait_recv()


def local(n_slab, n_mem, states, land_mask, cell_class, kappa, flow, obs_index, obs_values, obs_var):
    kd, rows, lon = states.shape
    ens = kd * n_mem
    n_pair, n_group, octs = n_slab // 2, 2 * n_mem, kd // 16
    n_obs = obs_index.shape[0]
    dma = pltpu.SemaphoreType.DMA
    vmem = pl.BlockSpec(memory_space=pltpu.VMEM)
    hbm = pl.BlockSpec(memory_space=pltpu.HBM)
    f32 = jnp.float32
    out = pl.pallas_call(
        functools.partial(cycle_kernel, n_slab, n_mem),
        out_shape=jax.ShapeDtypeStruct((rows, kd, lon), f32),
        in_specs=[hbm] * 8,
        out_specs=vmem,
        scratch_shapes=[
            pltpu.VMEM((2 * octs, 8, rows, lon), f32),
            pltpu.VMEM((octs, rows, 8, lon), f32),
            pltpu.SMEM(kappa.shape, f32),
            pltpu.SMEM(flow.shape, f32),
            dma((2 * octs,)), dma((2,)), dma((5,)),
            pltpu.VMEM((octs, 4 * rows, 8, lon), f32),
            pltpu.VMEM((octs, 4 * rows, 8, lon), f32),
            pltpu.VMEM((octs, 4 * rows, 8, lon), f32),
            pltpu.VMEM((4 * rows, 5, 8, lon), f32),
            pltpu.VMEM((4, 2, rows, lon), jnp.int32),
            pltpu.VMEM((2, 1, n_obs), jnp.int32),
            pltpu.VMEM((2, 2, 1, n_obs), f32),
            pltpu.VMEM((lon, 2 * n_obs), jnp.bfloat16),
            pltpu.VMEM((ens, 2 * n_obs), f32),
            pltpu.VMEM((ens // 2 + 8, ens), f32),
            pltpu.VMEM((n_pair, ens // 2 + 8, ens), f32),
            pltpu.VMEM((ens, ens), f32),
            pltpu.VMEM((ens, ens), f32),
            pltpu.VMEM((rows, ens, lon // 2), f32),
            pltpu.VMEM((rows, kd, lon // 2), f32),
            dma((3, 2)), dma((4, 2)), dma((3,)), dma((3,)), dma((octs, SPLIT)), dma((octs, SPLIT)),
            dma((octs,)), dma((octs,)), dma((octs, SPLIT)), dma((octs, SPLIT)), dma((octs,)),
            dma((n_group,)), dma((n_group,)), dma((n_pair,)), dma((n_pair,)), dma, dma,
            dma((octs, PARTS, n_group)), dma((octs, PARTS, n_group)), dma((PARTS,)), dma((PARTS,)),
        ],
        compiler_params=pltpu.CompilerParams(
            collective_id=0, has_side_effects=True, vmem_limit_bytes=48 * 1024 * 1024
        ),
        name="cycle",
    )(
        *(
            pltpu.with_memory_space_constraint(array, pltpu.HBM)
            for array in (
                states, cell_class, land_mask, kappa, flow,
                obs_index.reshape(1, n_obs), obs_values.reshape(1, n_obs), obs_var.reshape(1, n_obs),
            )
        )
    )
    return out.transpose(1, 0, 2)


def solution(mesh):
    return jax.shard_map(
        functools.partial(local, mesh.shape["slab"], mesh.shape["mem"]),
        mesh=mesh,
        in_specs=(
            P("mem", "slab", None),
            P("slab", None),
            P("slab", None),
            P(),
            P(),
            P("slab"),
            P("slab"),
            P("slab"),
        ),
        out_specs=P("mem", "slab", None),
        check_vma=False,
    )
```

```python
import functools

import jax
import jax.numpy as jnp
from jax import lax
from jax.experimental import pallas as pl
from jax.experimental.pallas import tpu as pltpu
from jax.sharding import PartitionSpec as P

STEPS = 8
ROOT_ITERATIONS = 8
NCLS = 8
HEIGHT = 8
SPLIT = 4
PARTS = 2


def halves(x):
    high = x.astype(jnp.bfloat16)
    return high, (x - high.astype(jnp.float32)).astype(jnp.bfloat16)


def left_parts(x):
    high, low = halves(x)
    return jnp.concatenate([high, high, low], axis=1)


def right_parts(x):
    high, low = halves(x)
    return jnp.concatenate([high, low, high], axis=0)


def product(left, right):
    return jnp.dot(left, right, preferred_element_type=jnp.float32)


def dot(a, b):
    return product(left_parts(a), right_parts(b))


def cycle_kernel(
    n_slab, n_mem,
    states_in, classes_in, mask_in, kappa_in, flow_in, obs_index, obs_values, obs_var,
    out,
    raw, states, kappa, flow, plane_sem, below_sem, above_sem, load_sem, table_sem, own_sem, land, odd, even, coef, geos, gobs, gval, pick, hxs, gpart, precv, gfull, turned, fore, mixed,
    geo_send, geo_recv, obs_send, obs_recv, y_send, y_recv, d_send, d_recv, r_send, r_recv, keep_sem,
    h_send, h_recv, p_send, p_recv, g_send, g_recv, a_send, a_recv, b_send, b_recv,
):
    s = lax.axis_index("slab")
    m = lax.axis_index("mem")
    q, y = lax.div(s, 2), lax.rem(s, 2)
    n_pair, n_group = n_slab // 2, 2 * n_mem
    octs, rows, lon = states.shape[0], states.shape[1], states.shape[3]
    half = lon // 2
    ens = fore.shape[1]
    n_obs = gobs.shape[2]
    line, core = lax.div(m, 2), lax.rem(m, 2)
    sibling = 2 * line + 1 - core
    kd = octs * 16
    group = y * n_mem + m
    last = n_pair - 1
    step_pair = 2 * y - 1

    def device(pair, side, member):
        return (2 * pair + side, member)

    def remote(src, dst, send, recv, where):
        return pltpu.make_async_remote_copy(
            src_ref=src, dst_ref=dst, send_sem=send, recv_sem=recv,
            device_id=where, device_id_type=pl.DeviceIdType.MESH,
        )

    def peer(k):
        other = lax.rem(group + k, n_group)
        return other, lax.div(other, n_mem), lax.rem(other, n_mem)

    def load(side, c):
        which = octs * side + c
        return pltpu.make_async_copy(
            states_in.at[pl.ds(pl.multiple_of(8 * which, 8), 8)], raw.at[which], load_sem.at[which]
        )

    own_loads = [
        pltpu.make_async_copy(classes_in, geos.at[1 + y, 0], own_sem.at[0]),
        pltpu.make_async_copy(mask_in, geos.at[1 + y, 1], own_sem.at[1]),
        pltpu.make_async_copy(obs_index, gobs.at[y], own_sem.at[2]),
        pltpu.make_async_copy(obs_values, gval.at[y, 0], own_sem.at[3]),
        pltpu.make_async_copy(obs_var, gval.at[y, 1], own_sem.at[4]),
    ]
    table_loads = [
        pltpu.make_async_copy(kappa_in, kappa, table_sem.at[0]),
        pltpu.make_async_copy(flow_in, flow, table_sem.at[1]),
    ]

    barrier = pltpu.get_barrier_semaphore()
    def tell(semaphore, where):
        pl.semaphore_signal(semaphore, inc=1, device_id=where, device_id_type=pl.DeviceIdType.MESH)

    across = 2 * (1 - line) + core
    tell(barrier, device(q, 1 - y, m))
    tell(barrier, device(q, y, sibling))
    tell(barrier, device(q, y, across))

    @pl.when(q > 0)
    def _():
        tell(barrier, device(q - 1, y, m))

    @pl.when(q < last)
    def _():
        tell(barrier, device(q + 1, y, m))

    for c in range(octs):
        load(1 - y, c).start()
    for c in range(octs):
        load(y, c).start()
    for copy in own_loads + table_loads:
        copy.start()
    for c in range(octs):
        load(1 - y, c).wait()
        states[c] = jnp.swapaxes(raw[octs * (1 - y) + c], 0, 1)
    for c in range(octs):
        load(y, c).wait()
        land[c, pl.ds(8 + 8 * y, 8)] = jnp.swapaxes(raw[octs * y + c], 0, 1)
    for copy in own_loads + table_loads:
        copy.wait()
    pl.semaphore_wait(barrier, 3 + jnp.where(q > 0, 1, 0) + jnp.where(q < last, 1, 0))

    def stage_tell(k):
        @pl.when((q > 0) & (q + k <= last))
        def _():
            tell(below_sem.at[k], device(q - 1, y, m))

        @pl.when((q < last) & (q - k >= 0))
        def _():
            tell(above_sem.at[k], device(q + 1, y, m))

    def stage_wait(k):
        @pl.when(q + 1 + k <= last)
        def _():
            pl.semaphore_wait(below_sem.at[k], 1)

        @pl.when(q - 1 - k >= 0)
        def _():
            pl.semaphore_wait(above_sem.at[k], 1)

    tell(plane_sem.at[0], device(q, 1 - y, m))
    if n_pair > 2:
        stage_tell(1)

    piece = 8 // SPLIT

    def y_copy(c, h):
        return remote(
            states.at[c, pl.ds(piece * h, piece)], land.at[c, pl.ds(8 + 8 * y + piece * h, piece)],
            y_send.at[c, h], y_recv.at[c, h], device(q, 1 - y, m),
        )

    def y_wait(c, h):
        return remote(
            states.at[c, pl.ds(0, piece)], land.at[c, pl.ds(16 - 8 * y + piece * h, piece)],
            y_send.at[c, h], y_recv.at[c, h], device(q, 1 - y, m),
        )

    def direct_copy(c):
        return remote(
            land.at[c, pl.ds(8 + 8 * y, 8)], land.at[c, pl.ds(24 * (1 - y), 8)],
            d_send.at[c], d_recv.at[c], device(q + step_pair, y, m),
        )

    def relay_copy(c, h):
        return remote(
            land.at[c, pl.ds(16 - 8 * y + piece * h, piece)], land.at[c, pl.ds(24 * y + piece * h, piece)],
            r_send.at[c, h], r_recv.at[c, h], device(q - step_pair, y, m),
        )

    fields = (geos.at[1 + y, 0], geos.at[1 + y, 1])

    def geo_pair(f):
        return remote(
            fields[f], geos.at[1 + y, f], geo_send.at[0, f], geo_recv.at[1 + y, f], device(q, 1 - y, m)
        )

    def geo_direct(f):
        return remote(
            fields[f], geos.at[3 * (1 - y), f], geo_send.at[1, f], geo_recv.at[3 * (1 - y), f],
            device(q + step_pair, y, m),
        )

    def geo_relay(f):
        return remote(
            geos.at[2 - y, f], geos.at[3 * y, f], geo_send.at[2, f], geo_recv.at[3 * y, f],
            device(q - step_pair, y, m),
        )

    def geo_wait(slot, f):
        return remote(fields[f], geos.at[slot, f], geo_send.at[0, f], geo_recv.at[slot, f], device(q, 1 - y, m))

    observed = (gobs.at[y], gval.at[y, 0], gval.at[y, 1])
    other_observed = (gobs.at[1 - y], gval.at[1 - y, 0], gval.at[1 - y, 1])

    def obs_copy(f):
        return remote(observed[f], observed[f], obs_send.at[f], obs_recv.at[f], device(q, 1 - y, m))

    def obs_wait(f):
        return remote(other_observed[f], other_observed[f], obs_send.at[f], obs_recv.at[f], device(q, 1 - y, m))

    forward_edge = (q + step_pair >= 0) & (q + step_pair <= last)
    backward_edge = (q - step_pair >= 0) & (q - step_pair <= last)

    for f in range(2):
        geo_pair(f).start()
    for f in range(3):
        obs_copy(f).start()
    for c in range(octs):
        for h in range(SPLIT):
            y_copy(c, h).start()

    @pl.when(forward_edge)
    def _():
        for f in range(2):
            geo_direct(f).start()
        for c in range(octs):
            direct_copy(c).start()

    @pl.when(q == 0)
    def _():
        geos[0] = jnp.zeros(geos.shape[1:], jnp.int32)
        for c in range(octs):
            land[c, 0:8] = jnp.zeros((8, 8, lon), jnp.float32)

    @pl.when(q == last)
    def _():
        geos[3] = jnp.zeros(geos.shape[1:], jnp.int32)
        for c in range(octs):
            land[c, 24:32] = jnp.zeros((8, 8, lon), jnp.float32)

    for f in range(2):
        geo_wait(2 - y, f).wait_recv()

    @pl.when(backward_edge)
    def _():
        for f in range(2):
            geo_relay(f).start()
            geo_wait(3 * (1 - y), f).wait_recv()

    pl.semaphore_wait(plane_sem.at[0], 1)
    tell(plane_sem.at[1], device(q, y, across))
    lane = lax.broadcasted_iota(jnp.int32, (8, lon), 1)

    def coefficients(k, carry):
        classes = geos[k, 0]
        wet = geos[k, 1].astype(jnp.float32)
        diffusion = jnp.zeros(classes.shape, jnp.float32)
        east = jnp.zeros(classes.shape, jnp.float32)
        north = jnp.zeros(classes.shape, jnp.float32)
        for label in range(NCLS):
            hit = classes == label
            diffusion = jnp.where(hit, kappa[label], diffusion)
            east = jnp.where(hit, flow[0, label], east)
            north = jnp.where(hit, flow[1, label], north)
        terms = (
            wet * (1.0 - 4.0 * diffusion),
            wet * (diffusion - 0.5 * north),
            wet * (diffusion + 0.5 * north),
            jnp.where(lane == lon - 1, 0.0, wet * (diffusion - 0.5 * east)),
            jnp.where(lane == 0, 0.0, wet * (diffusion + 0.5 * east)),
        )
        for index, term in enumerate(terms):
            for row in range(8):
                coef[8 * k + row, index] = jnp.broadcast_to(term[row : row + 1], (8, lon))
        return carry

    lax.fori_loop(1 - y, 4 - y, coefficients, 0)

    for f in range(3):
        obs_wait(f).wait_recv()
    place = jnp.concatenate([gobs[0], gobs[1]], axis=1)
    column = place & (lon - 1)
    pick[...] = jnp.where(
        lax.broadcasted_iota(jnp.int32, (lon, 2 * n_obs), 0) == column, 1.0, 0.0
    ).astype(jnp.bfloat16)
    side = lax.div(lax.broadcasted_iota(jnp.int32, (1, 2 * n_obs), 1), n_obs)
    obs_row = rows * side + (place >> (lon.bit_length() - 1))

    @pl.when(forward_edge)
    def _():
        for f in range(2):
            geo_wait(3 * y, f).wait_recv()

    lax.fori_loop(3 * y, 3 * y + 1, coefficients, 0)

    def relay(c, h):
        y_wait(c, h).wait_recv()

        @pl.when(backward_edge)
        def _():
            relay_copy(c, h).start()

    def advance(c, source, target, height, base):
        level = [source[c, base - 1], source[c, base]]
        for k in range(height):
            level.append(source[c, base + k + 1])
            south, center, north = level[k : k + 3]
            target[c, base + k] = (
                coef[base + k, 0] * center
                + coef[base + k, 1] * north
                + coef[base + k, 2] * south
                + coef[base + k, 3] * pltpu.roll(center, lon - 1, 1)
                + coef[base + k, 4] * pltpu.roll(center, 1, 1)
            )

    def rows_at(step, c, first, count):
        source = land if step == 1 else (odd, even)[step % 2]
        target = (even, odd)[step % 2]

        def some(g, inner):
            advance(c, source, target, HEIGHT, first + HEIGHT * g)
            return inner

        full = count // HEIGHT
        if full > 1:
            lax.fori_loop(0, full, some, 0)
        elif full == 1:
            some(0, 0)
        if count % HEIGHT:
            advance(c, source, target, count % HEIGHT, first + HEIGHT * full)

    def early(c):
        for step in range(1, STEPS + 1):
            rows_at(step, c, step + 8 * (1 - y), 24 - 2 * step)

    def late(c):
        for step in range(1, STEPS + 1):
            rows_at(step, c, step + y * (24 - 2 * step), 8)

    def direct_arrived(c):
        @pl.when(backward_edge)
        def _():
            remote(states.at[c], land.at[c, pl.ds(24 * (1 - y), 8)], d_send.at[c], d_recv.at[c], device(q, 1 - y, m)).wait_recv()

    def relay_arrived(c):
        @pl.when(forward_edge)
        def _():
            for h in range(SPLIT):
                remote(
                    states.at[c, pl.ds(0, piece)], land.at[c, pl.ds(24 * y + piece * h, piece)],
                    r_send.at[c, h], r_recv.at[c, h], device(q, 1 - y, m),
                ).wait_recv()

    deep = rows // PARTS

    def a_copy(c, h, other, ty, tm):
        return remote(
            even.at[c, pl.ds(8 + 8 * ty + deep * h, deep), :, pl.ds(pl.multiple_of(half * lax.rem(tm, 2), 128), half)],
            fore.at[pl.ds(deep * h, deep), pl.ds(pl.multiple_of(kd * m + 8 * octs * y + 8 * c, 8), 8), :],
            a_send.at[c, h, other], a_recv.at[c, h, group], device(q, ty, tm),
        )

    def a_wait(c, h, other, ty, tm):
        return remote(
            even.at[c, pl.ds(8, deep), :, pl.ds(0, half)],
            fore.at[pl.ds(deep * h, deep), pl.ds(pl.multiple_of(kd * tm + 8 * octs * ty + 8 * c, 8), 8), :],
            a_send.at[c, h, other], a_recv.at[c, h, other], device(q, ty, tm),
        )

    def a_keep(c, h):
        return pltpu.make_async_copy(
            even.at[c, pl.ds(8 + 8 * y + deep * h, deep), :, pl.ds(pl.multiple_of(half * core, 128), half)],
            fore.at[pl.ds(deep * h, deep), pl.ds(pl.multiple_of(kd * m + 8 * octs * y + 8 * c, 8), 8), :],
            a_send.at[c, h, group],
        )

    def far_start(c, h):
        for k in range(n_mem):
            tm = lax.rem(m + 2 + k, n_mem)
            a_copy(c, h, (1 - y) * n_mem + tm, 1 - y, tm).start()

    def near_start(c, h):
        for k in range(1, n_mem):
            tm = lax.rem(m + k, n_mem)
            a_copy(c, h, y * n_mem + tm, y, tm).start()
        a_keep(c, h).start()

    own_rows = kd * m + 8 * octs * y

    def observe(c):
        rest = even[c, 8:24].reshape(16 * 8, lon)
        pieces = []
        for _ in range(3):
            part = rest.astype(jnp.bfloat16)
            pieces.append(part)
            rest = rest - part.astype(jnp.float32)
        seen = jnp.dot(jnp.concatenate(pieces, axis=0), pick[...], preferred_element_type=jnp.float32)
        seen = seen[:128] + seen[128:256] + seen[256:]
        hx = jnp.zeros((8, 2 * n_obs), jnp.float32)
        for row in range(2 * rows):
            hx = hx + jnp.where(obs_row == row, seen[8 * row : 8 * row + 8], 0.0)
        hxs[pl.ds(pl.multiple_of(own_rows + 8 * c, 8), 8)] = hx

    for h in range(SPLIT):
        relay(0, h)
    direct_arrived(0)
    early(0)
    pl.semaphore_wait(plane_sem.at[1], 1)
    far_start(0, 0)
    for c in range(octs):
        if c < octs - 1:
            for h in range(SPLIT // 2):
                relay(c + 1, h)
        relay_arrived(c)
        late(c)
        if c < octs - 1:
            for h in range(PARTS):
                near_start(c, h)
            for h in range(SPLIT // 2, SPLIT):
                relay(c + 1, h)
            direct_arrived(c + 1)
            early(c + 1)
            observe(c)
    observe(octs - 1)
    if n_pair > 2:
        stage_wait(1)
    if n_pair > 3:
        stage_tell(2)

    mine = pl.ds(pl.multiple_of(own_rows, 8), 8 * octs)

    def h_copy(other, ty, tm):
        return remote(hxs.at[mine], hxs.at[mine], h_send.at[other], h_recv.at[group], device(q, ty, tm))

    def h_wait(other, ty, tm):
        there = hxs.at[pl.ds(pl.multiple_of(kd * tm + 8 * octs * ty, 8), 8 * octs)]
        return remote(there, there, h_send.at[other], h_recv.at[other], device(q, ty, tm))

    for k in range(1, n_group):
        h_copy(*peer(k)).start()
    for h in range(PARTS):
        for c in range(octs):
            if h > 0 or c > 0:
                far_start(c, h)
        for c in range(1, octs):
            near_start(c, h)
    for k in range(1, n_group):
        h_wait(*peer(k)).wait_recv()

    share = ens // 2
    full = hxs[...]
    ybar = jnp.sum(full, axis=0, keepdims=True) / ens
    slab = (2 * q + side).astype(jnp.float32)
    err = jnp.concatenate([gval[0, 1], gval[1, 1]], axis=1) * (1.0 + 2.0 * slab / float(n_slab - 1))
    scaled = jnp.sqrt(err * (ens - 1.0))
    anom = (full - ybar) / scaled
    part = (hxs[pl.ds(pl.multiple_of(share * core, 8), share)] - ybar) / scaled
    dev = (jnp.concatenate([gval[0, 0], gval[1, 0]], axis=1) - ybar) / jnp.sqrt(err)
    both = jnp.concatenate([part, jnp.broadcast_to(dev, (16, 2 * n_obs))], axis=0)
    high, low = halves(anom)
    sums = lax.dot_general(
        left_parts(both), jnp.concatenate([high, low, high], axis=1), (((1,), (1,)), ((), ())),
        preferred_element_type=jnp.float32,
    )
    gpart[...] = sums[: share + 8]

    def p_copy(k):
        tq = lax.rem(q + k, n_pair)
        return remote(gpart, precv.at[q], p_send.at[tq], p_recv.at[q], device(tq, y, m))

    def p_wait(k):
        tq = lax.rem(q + k, n_pair)
        return remote(gpart, precv.at[tq], p_send.at[tq], p_recv.at[tq], device(tq, y, m))

    for k in range(2, n_pair - 1):
        if k > 2:
            stage_tell(k)
        stage_wait(k)
    for k in range(1, n_pair):
        p_copy(k).start()
    precv[q] = sums[: share + 8]
    for k in range(1, n_pair):
        p_wait(k).wait_recv()
    total = precv[0]
    for k in range(1, n_pair):
        total = total + precv[k]
    own = pl.ds(pl.multiple_of(share * core, 8), share)
    theirs = pl.ds(pl.multiple_of(share * (1 - core), 8), share)
    gfull[own] = total[:share]
    g_copy = remote(gfull.at[own], gfull.at[own], g_send, g_recv, device(q, y, sibling))
    g_copy.start()
    proj = jnp.concatenate([total[share:], total[share:]], axis=0)
    remote(gfull.at[theirs], gfull.at[theirs], g_send, g_recv, device(q, y, sibling)).wait_recv()

    ident = jnp.where(
        lax.broadcasted_iota(jnp.int32, (ens, ens), 0) == lax.broadcasted_iota(jnp.int32, (ens, ens), 1), 1.0, 0.0
    )
    matrix = ident + gfull[...]
    scale = jnp.sum(jnp.sum(matrix * ident, axis=1, keepdims=True), axis=0, keepdims=True)

    upper = matrix / scale
    factor = 1.5 * ident - 0.5 * upper
    upper, lower = dot(upper, factor), factor
    for turn in range(ROOT_ITERATIONS - 1):
        factor = 1.5 * ident - 0.5 * dot(lower, upper)
        if turn < ROOT_ITERATIONS - 2:
            upper = dot(upper, factor)
        lower = dot(factor, lower)
    high, low = halves(proj)
    once = lax.dot_general(
        left_parts(lower), jnp.concatenate([high, low, high], axis=1), (((1,), (1,)), ((), ())),
        preferred_element_type=jnp.float32,
    )
    mean_w = dot(lower, once)[:, :1] / (scale * jnp.sqrt(jnp.float32(ens - 1.0)))
    total_w = lower / jnp.sqrt(scale) + mean_w
    omega = 1.0 / ens + total_w - jnp.sum(total_w, axis=0, keepdims=True) / ens
    turned[...] = omega.T
    weights = left_parts(
        jnp.concatenate(
            [turned[pl.ds(pl.multiple_of(kd * m, 8), kd)], turned[pl.ds(pl.multiple_of(kd * sibling, 8), kd)]], axis=0
        )
    )

    def b_copy(h):
        return remote(
            mixed.at[pl.ds(deep * h, deep)],
            out.at[pl.ds(deep * h, deep), :, pl.ds(pl.multiple_of(half * core, 128), half)],
            b_send.at[h], b_recv.at[h], device(q, y, sibling),
        )

    def b_wait(h):
        return remote(
            mixed.at[pl.ds(deep * h, deep)],
            out.at[pl.ds(deep * h, deep), :, pl.ds(pl.multiple_of(half * (1 - core), 128), half)],
            b_send.at[h], b_recv.at[h], device(q, y, sibling),
        )

    for h in range(PARTS):
        for c in range(octs):
            a_keep(c, h).wait()
            for k in range(1, n_group):
                a_wait(c, h, *peer(k)).wait_recv()
        for row in range(deep * h, deep * h + deep):
            result = product(weights, right_parts(fore[row]))
            mixed[row] = result[kd:]
            out[row, :, pl.ds(pl.multiple_of(half * core, 128), half)] = result[:kd]
        b_copy(h).start()

    for f in range(2):
        geo_pair(f).wait_send()
    for f in range(3):
        obs_copy(f).wait_send()
    for c in range(octs):
        for h in range(SPLIT):
            y_copy(c, h).wait_send()

    @pl.when(forward_edge)
    def _():
        for f in range(2):
            geo_direct(f).wait_send()
        for c in range(octs):
            direct_copy(c).wait_send()

    @pl.when(backward_edge)
    def _():
        for f in range(2):
            geo_relay(f).wait_send()
        for c in range(octs):
            for h in range(SPLIT):
                relay_copy(c, h).wait_send()

    for k in range(1, n_group):
        for c in range(octs):
            for h in range(PARTS):
                a_copy(c, h, *peer(k)).wait_send()
        h_copy(*peer(k)).wait_send()
    for k in range(1, n_pair):
        p_copy(k).wait_send()
    g_copy.wait_send()
    for h in range(PARTS):
        b_copy(h).wait_send()
        b_wait(h).wait_recv()


def local(n_slab, n_mem, states, land_mask, cell_class, kappa, flow, obs_index, obs_values, obs_var):
    kd, rows, lon = states.shape
    ens = kd * n_mem
    n_pair, n_group, octs = n_slab // 2, 2 * n_mem, kd // 16
    n_obs = obs_index.shape[0]
    dma = pltpu.SemaphoreType.DMA
    vmem = pl.BlockSpec(memory_space=pltpu.VMEM)
    hbm = pl.BlockSpec(memory_space=pltpu.HBM)
    f32 = jnp.float32
    out = pl.pallas_call(
        functools.partial(cycle_kernel, n_slab, n_mem),
        out_shape=jax.ShapeDtypeStruct((rows, kd, lon), f32),
        in_specs=[hbm] * 8,
        out_specs=vmem,
        scratch_shapes=[
            pltpu.VMEM((2 * octs, 8, rows, lon), f32),
            pltpu.VMEM((octs, rows, 8, lon), f32),
            pltpu.SMEM(kappa.shape, f32),
            pltpu.SMEM(flow.shape, f32),
            pltpu.SemaphoreType.REGULAR((2,)), pltpu.SemaphoreType.REGULAR((n_pair,)), pltpu.SemaphoreType.REGULAR((n_pair,)),
            dma((2 * octs,)), dma((2,)), dma((5,)),
            pltpu.VMEM((octs, 4 * rows, 8, lon), f32),
            pltpu.VMEM((octs, 4 * rows, 8, lon), f32),
            pltpu.VMEM((octs, 4 * rows, 8, lon), f32),
            pltpu.VMEM((4 * rows, 5, 8, lon), f32),
            pltpu.VMEM((4, 2, rows, lon), jnp.int32),
            pltpu.VMEM((2, 1, n_obs), jnp.int32),
            pltpu.VMEM((2, 2, 1, n_obs), f32),
            pltpu.VMEM((lon, 2 * n_obs), jnp.bfloat16),
            pltpu.VMEM((ens, 2 * n_obs), f32),
            pltpu.VMEM((ens // 2 + 8, ens), f32),
            pltpu.VMEM((n_pair, ens // 2 + 8, ens), f32),
            pltpu.VMEM((ens, ens), f32),
            pltpu.VMEM((ens, ens), f32),
            pltpu.VMEM((rows, ens, lon // 2), f32),
            pltpu.VMEM((rows, kd, lon // 2), f32),
            dma((3, 2)), dma((4, 2)), dma((3,)), dma((3,)), dma((octs, SPLIT)), dma((octs, SPLIT)),
            dma((octs,)), dma((octs,)), dma((octs, SPLIT)), dma((octs, SPLIT)), dma((octs,)),
            dma((n_group,)), dma((n_group,)), dma((n_pair,)), dma((n_pair,)), dma, dma,
            dma((octs, PARTS, n_group)), dma((octs, PARTS, n_group)), dma((PARTS,)), dma((PARTS,)),
        ],
        compiler_params=pltpu.CompilerParams(
            collective_id=0, has_side_effects=True, vmem_limit_bytes=48 * 1024 * 1024
        ),
        name="cycle",
    )(
        *(
            pltpu.with_memory_space_constraint(array, pltpu.HBM)
            for array in (
                states, cell_class, land_mask, kappa, flow,
                obs_index.reshape(1, n_obs), obs_values.reshape(1, n_obs), obs_var.reshape(1, n_obs),
            )
        )
    )
    return out.transpose(1, 0, 2)


def solution(mesh):
    return jax.shard_map(
        functools.partial(local, mesh.shape["slab"], mesh.shape["mem"]),
        mesh=mesh,
        in_specs=(
            P("mem", "slab", None),
            P("slab", None),
            P("slab", None),
            P(),
            P(),
            P("slab"),
            P("slab"),
            P("slab"),
        ),
        out_specs=P("mem", "slab", None),
        check_vma=False,
    )
```

```python
import functools

import jax
import jax.numpy as jnp
from jax import lax
from jax.experimental import pallas as pl
from jax.experimental.pallas import tpu as pltpu
from jax.sharding import PartitionSpec as P

STEPS = 8
ROOT_ITERATIONS = 8
NCLS = 8
HEIGHT = 8
SPLIT = 4
PARTS = 2


def halves(x):
    high = x.astype(jnp.bfloat16)
    return high, (x - high.astype(jnp.float32)).astype(jnp.bfloat16)


def left_parts(x):
    high, low = halves(x)
    return jnp.concatenate([high, high, low], axis=1)


def right_parts(x):
    high, low = halves(x)
    return jnp.concatenate([high, low, high], axis=0)


def product(left, right):
    return jnp.dot(left, right, preferred_element_type=jnp.float32)


def dot(a, b):
    return product(left_parts(a), right_parts(b))


def cycle_kernel(
    n_slab, n_mem,
    states_in, classes_in, mask_in, kappa_in, flow_in, obs_index, obs_values, obs_var,
    out,
    raw, states, kappa, flow, plane_sem, below_sem, above_sem, load_sem, table_sem, own_sem, land, odd, even, coef, geos, gobs, gval, pick, hxs, gpart, precv, gfull, turned, fore, mixed,
    geo_send, geo_recv, obs_send, obs_recv, y_send, y_recv, d_send, d_recv, r_send, r_recv, keep_sem,
    h_send, h_recv, p_send, p_recv, g_send, g_recv, a_send, a_recv, b_send, b_recv,
):
    s = lax.axis_index("slab")
    m = lax.axis_index("mem")
    q, y = lax.div(s, 2), lax.rem(s, 2)
    n_pair, n_group = n_slab // 2, 2 * n_mem
    octs, rows, lon = states.shape[0], states.shape[1], states.shape[3]
    half = lon // 2
    ens = fore.shape[1]
    n_obs = gobs.shape[2]
    line, core = lax.div(m, 2), lax.rem(m, 2)
    sibling = 2 * line + 1 - core
    kd = octs * 16
    group = y * n_mem + m
    last = n_pair - 1
    step_pair = 2 * y - 1

    def device(pair, side, member):
        return (2 * pair + side, member)

    def remote(src, dst, send, recv, where):
        return pltpu.make_async_remote_copy(
            src_ref=src, dst_ref=dst, send_sem=send, recv_sem=recv,
            device_id=where, device_id_type=pl.DeviceIdType.MESH,
        )

    def peer(k):
        other = lax.rem(group + k, n_group)
        return other, lax.div(other, n_mem), lax.rem(other, n_mem)

    def load(side, c):
        which = octs * side + c
        return pltpu.make_async_copy(
            states_in.at[pl.ds(pl.multiple_of(8 * which, 8), 8)], raw.at[which], load_sem.at[which]
        )

    own_loads = [
        pltpu.make_async_copy(classes_in, geos.at[1 + y, 0], own_sem.at[0]),
        pltpu.make_async_copy(mask_in, geos.at[1 + y, 1], own_sem.at[1]),
        pltpu.make_async_copy(obs_index, gobs.at[y], own_sem.at[2]),
        pltpu.make_async_copy(obs_values, gval.at[y, 0], own_sem.at[3]),
        pltpu.make_async_copy(obs_var, gval.at[y, 1], own_sem.at[4]),
    ]
    table_loads = [
        pltpu.make_async_copy(kappa_in, kappa, table_sem.at[0]),
        pltpu.make_async_copy(flow_in, flow, table_sem.at[1]),
    ]

    barrier = pltpu.get_barrier_semaphore()
    def tell(semaphore, where):
        pl.semaphore_signal(semaphore, inc=1, device_id=where, device_id_type=pl.DeviceIdType.MESH)

    across = 2 * (1 - line) + core
    tell(barrier, device(q, 1 - y, m))
    tell(barrier, device(q, y, sibling))
    tell(barrier, device(q, y, across))

    @pl.when(q > 0)
    def _():
        tell(barrier, device(q - 1, y, m))

    @pl.when(q < last)
    def _():
        tell(barrier, device(q + 1, y, m))

    for c in range(octs):
        load(1 - y, c).start()
    for c in range(octs):
        load(y, c).start()
    for copy in own_loads + table_loads:
        copy.start()
    for c in range(octs):
        load(1 - y, c).wait()
        states[c] = jnp.swapaxes(raw[octs * (1 - y) + c], 0, 1)
    for c in range(octs):
        load(y, c).wait()
        land[c, pl.ds(8 + 8 * y, 8)] = jnp.swapaxes(raw[octs * y + c], 0, 1)
    for copy in own_loads + table_loads:
        copy.wait()
    pl.semaphore_wait(barrier, 3 + jnp.where(q > 0, 1, 0) + jnp.where(q < last, 1, 0))

    def stage_tell(k):
        @pl.when((q > 0) & (q + k <= last))
        def _():
            tell(below_sem.at[k], device(q - 1, y, m))

        @pl.when((q < last) & (q - k >= 0))
        def _():
            tell(above_sem.at[k], device(q + 1, y, m))

    def stage_wait(k):
        @pl.when(q + 1 + k <= last)
        def _():
            pl.semaphore_wait(below_sem.at[k], 1)

        @pl.when(q - 1 - k >= 0)
        def _():
            pl.semaphore_wait(above_sem.at[k], 1)

    tell(plane_sem.at[0], device(q, 1 - y, m))
    if n_pair > 2:
        stage_tell(1)

    piece = 8 // SPLIT

    def y_copy(c, h):
        return remote(
            states.at[c, pl.ds(piece * h, piece)], land.at[c, pl.ds(8 + 8 * y + piece * h, piece)],
            y_send.at[c, h], y_recv.at[c, h], device(q, 1 - y, m),
        )

    def y_wait(c, h):
        return remote(
            states.at[c, pl.ds(0, piece)], land.at[c, pl.ds(16 - 8 * y + piece * h, piece)],
            y_send.at[c, h], y_recv.at[c, h], device(q, 1 - y, m),
        )

    def direct_copy(c):
        return remote(
            land.at[c, pl.ds(8 + 8 * y, 8)], land.at[c, pl.ds(24 * (1 - y), 8)],
            d_send.at[c], d_recv.at[c], device(q + step_pair, y, m),
        )

    def relay_copy(c, h):
        return remote(
            land.at[c, pl.ds(16 - 8 * y + piece * h, piece)], land.at[c, pl.ds(24 * y + piece * h, piece)],
            r_send.at[c, h], r_recv.at[c, h], device(q - step_pair, y, m),
        )

    fields = (geos.at[1 + y, 0], geos.at[1 + y, 1])

    def geo_pair(f):
        return remote(
            fields[f], geos.at[1 + y, f], geo_send.at[0, f], geo_recv.at[1 + y, f], device(q, 1 - y, m)
        )

    def geo_direct(f):
        return remote(
            fields[f], geos.at[3 * (1 - y), f], geo_send.at[1, f], geo_recv.at[3 * (1 - y), f],
            device(q + step_pair, y, m),
        )

    def geo_relay(f):
        return remote(
            geos.at[2 - y, f], geos.at[3 * y, f], geo_send.at[2, f], geo_recv.at[3 * y, f],
            device(q - step_pair, y, m),
        )

    def geo_wait(slot, f):
        return remote(fields[f], geos.at[slot, f], geo_send.at[0, f], geo_recv.at[slot, f], device(q, 1 - y, m))

    observed = (gobs.at[y], gval.at[y, 0], gval.at[y, 1])
    other_observed = (gobs.at[1 - y], gval.at[1 - y, 0], gval.at[1 - y, 1])

    def obs_copy(f):
        return remote(observed[f], observed[f], obs_send.at[f], obs_recv.at[f], device(q, 1 - y, m))

    def obs_wait(f):
        return remote(other_observed[f], other_observed[f], obs_send.at[f], obs_recv.at[f], device(q, 1 - y, m))

    forward_edge = (q + step_pair >= 0) & (q + step_pair <= last)
    backward_edge = (q - step_pair >= 0) & (q - step_pair <= last)

    for f in range(2):
        geo_pair(f).start()
    for f in range(3):
        obs_copy(f).start()
    for c in range(octs):
        for h in range(SPLIT):
            y_copy(c, h).start()

    @pl.when(forward_edge)
    def _():
        for f in range(2):
            geo_direct(f).start()
        for c in range(octs):
            direct_copy(c).start()

    @pl.when(q == 0)
    def _():
        geos[0] = jnp.zeros(geos.shape[1:], jnp.int32)
        for c in range(octs):
            land[c, 0:8] = jnp.zeros((8, 8, lon), jnp.float32)

    @pl.when(q == last)
    def _():
        geos[3] = jnp.zeros(geos.shape[1:], jnp.int32)
        for c in range(octs):
            land[c, 24:32] = jnp.zeros((8, 8, lon), jnp.float32)

    for f in range(2):
        geo_wait(2 - y, f).wait_recv()

    @pl.when(backward_edge)
    def _():
        for f in range(2):
            geo_relay(f).start()
            geo_wait(3 * (1 - y), f).wait_recv()

    pl.semaphore_wait(plane_sem.at[0], 1)
    tell(plane_sem.at[1], device(q, y, across))
    lane = lax.broadcasted_iota(jnp.int32, (8, lon), 1)

    def coefficients(k, carry):
        classes = geos[k, 0]
        wet = geos[k, 1].astype(jnp.float32)
        diffusion = jnp.zeros(classes.shape, jnp.float32)
        east = jnp.zeros(classes.shape, jnp.float32)
        north = jnp.zeros(classes.shape, jnp.float32)
        for label in range(NCLS):
            hit = classes == label
            diffusion = jnp.where(hit, kappa[label], diffusion)
            east = jnp.where(hit, flow[0, label], east)
            north = jnp.where(hit, flow[1, label], north)
        terms = (
            wet * (1.0 - 4.0 * diffusion),
            wet * (diffusion - 0.5 * north),
            wet * (diffusion + 0.5 * north),
            jnp.where(lane == lon - 1, 0.0, wet * (diffusion - 0.5 * east)),
            jnp.where(lane == 0, 0.0, wet * (diffusion + 0.5 * east)),
        )
        for index, term in enumerate(terms):
            for row in range(8):
                coef[8 * k + row, index] = jnp.broadcast_to(term[row : row + 1], (8, lon))
        return carry

    lax.fori_loop(1 - y, 4 - y, coefficients, 0)

    for f in range(3):
        obs_wait(f).wait_recv()
    place = jnp.concatenate([gobs[0], gobs[1]], axis=1)
    column = place & (lon - 1)
    pick[...] = jnp.where(
        lax.broadcasted_iota(jnp.int32, (lon, 2 * n_obs), 0) == column, 1.0, 0.0
    ).astype(jnp.bfloat16)
    side = lax.div(lax.broadcasted_iota(jnp.int32, (1, 2 * n_obs), 1), n_obs)
    obs_row = rows * side + (place >> (lon.bit_length() - 1))

    @pl.when(forward_edge)
    def _():
        for f in range(2):
            geo_wait(3 * y, f).wait_recv()

    lax.fori_loop(3 * y, 3 * y + 1, coefficients, 0)

    def relay(c, h):
        y_wait(c, h).wait_recv()

        @pl.when(backward_edge)
        def _():
            relay_copy(c, h).start()

    def advance(c, source, target, height, base):
        level = [source[c, base - 1], source[c, base]]
        for k in range(height):
            level.append(source[c, base + k + 1])
            south, center, north = level[k : k + 3]
            target[c, base + k] = (
                coef[base + k, 0] * center
                + coef[base + k, 1] * north
                + coef[base + k, 2] * south
                + coef[base + k, 3] * pltpu.roll(center, lon - 1, 1)
                + coef[base + k, 4] * pltpu.roll(center, 1, 1)
            )

    def rows_at(step, c, first, count):
        source = land if step == 1 else (odd, even)[step % 2]
        target = (even, odd)[step % 2]

        def some(g, inner):
            advance(c, source, target, HEIGHT, first + HEIGHT * g)
            return inner

        full = count // HEIGHT
        if full > 1:
            lax.fori_loop(0, full, some, 0)
        elif full == 1:
            some(0, 0)
        if count % HEIGHT:
            advance(c, source, target, count % HEIGHT, first + HEIGHT * full)

    def early(c):
        for step in range(1, STEPS + 1):
            rows_at(step, c, step + 8 * (1 - y), 24 - 2 * step)

    def late(c):
        for step in range(1, STEPS + 1):
            rows_at(step, c, step + y * (24 - 2 * step), 8)

    def direct_arrived(c):
        @pl.when(backward_edge)
        def _():
            remote(states.at[c], land.at[c, pl.ds(24 * (1 - y), 8)], d_send.at[c], d_recv.at[c], device(q, 1 - y, m)).wait_recv()

    def relay_arrived(c):
        @pl.when(forward_edge)
        def _():
            for h in range(SPLIT):
                remote(
                    states.at[c, pl.ds(0, piece)], land.at[c, pl.ds(24 * y + piece * h, piece)],
                    r_send.at[c, h], r_recv.at[c, h], device(q, 1 - y, m),
                ).wait_recv()

    deep = rows // PARTS

    def a_copy(c, h, other, ty, tm):
        return remote(
            even.at[c, pl.ds(8 + 8 * ty + deep * h, deep), :, pl.ds(pl.multiple_of(half * lax.rem(tm, 2), 128), half)],
            fore.at[pl.ds(deep * h, deep), pl.ds(pl.multiple_of(kd * m + 8 * octs * y + 8 * c, 8), 8), :],
            a_send.at[c, h, other], a_recv.at[c, h, group], device(q, ty, tm),
        )

    def a_wait(c, h, other, ty, tm):
        return remote(
            even.at[c, pl.ds(8, deep), :, pl.ds(0, half)],
            fore.at[pl.ds(deep * h, deep), pl.ds(pl.multiple_of(kd * tm + 8 * octs * ty + 8 * c, 8), 8), :],
            a_send.at[c, h, other], a_recv.at[c, h, other], device(q, ty, tm),
        )

    def a_keep(c, h):
        return pltpu.make_async_copy(
            even.at[c, pl.ds(8 + 8 * y + deep * h, deep), :, pl.ds(pl.multiple_of(half * core, 128), half)],
            fore.at[pl.ds(deep * h, deep), pl.ds(pl.multiple_of(kd * m + 8 * octs * y + 8 * c, 8), 8), :],
            a_send.at[c, h, group],
        )

    def far_start(c, h):
        for k in range(n_mem):
            tm = lax.rem(m + 2 + k, n_mem)
            a_copy(c, h, (1 - y) * n_mem + tm, 1 - y, tm).start()

    def near_start(c, h):
        for k in range(1, n_mem):
            tm = lax.rem(m + k, n_mem)
            a_copy(c, h, y * n_mem + tm, y, tm).start()
        a_keep(c, h).start()

    own_rows = kd * m + 8 * octs * y

    def observe(c):
        rest = even[c, 8:24].reshape(16 * 8, lon)
        pieces = []
        for _ in range(3):
            part = rest.astype(jnp.bfloat16)
            pieces.append(part)
            rest = rest - part.astype(jnp.float32)
        seen = jnp.dot(jnp.concatenate(pieces, axis=0), pick[...], preferred_element_type=jnp.float32)
        seen = seen[:128] + seen[128:256] + seen[256:]
        hx = jnp.zeros((8, 2 * n_obs), jnp.float32)
        for row in range(2 * rows):
            hx = hx + jnp.where(obs_row == row, seen[8 * row : 8 * row + 8], 0.0)
        hxs[pl.ds(pl.multiple_of(own_rows + 8 * c, 8), 8)] = hx

    for h in range(SPLIT):
        relay(0, h)
    direct_arrived(0)
    early(0)
    pl.semaphore_wait(plane_sem.at[1], 1)
    far_start(0, 0)
    for c in range(octs):
        if c < octs - 1:
            for h in range(SPLIT // 2):
                relay(c + 1, h)
        relay_arrived(c)
        late(c)
        if c < octs - 1:
            for h in range(PARTS):
                near_start(c, h)
            for h in range(SPLIT // 2, SPLIT):
                relay(c + 1, h)
            direct_arrived(c + 1)
            early(c + 1)
            observe(c)
    observe(octs - 1)
    if n_pair > 2:
        stage_wait(1)
    if n_pair > 3:
        stage_tell(2)

    mine = pl.ds(pl.multiple_of(own_rows, 8), 8 * octs)

    def h_copy(other, ty, tm):
        return remote(hxs.at[mine], hxs.at[mine], h_send.at[other], h_recv.at[group], device(q, ty, tm))

    def h_wait(other, ty, tm):
        there = hxs.at[pl.ds(pl.multiple_of(kd * tm + 8 * octs * ty, 8), 8 * octs)]
        return remote(there, there, h_send.at[other], h_recv.at[other], device(q, ty, tm))

    for k in range(1, n_group):
        h_copy(*peer(k)).start()
    for h in range(PARTS):
        for c in range(octs):
            if c > 0:
                far_start(c, h)
        if h == 0:
            far_start(0, 1)
        for c in range(1, octs):
            near_start(c, h)
    for k in range(1, n_group):
        h_wait(*peer(k)).wait_recv()

    share = ens // 2
    full = hxs[...]
    ybar = jnp.sum(full, axis=0, keepdims=True) / ens
    slab = (2 * q + side).astype(jnp.float32)
    err = jnp.concatenate([gval[0, 1], gval[1, 1]], axis=1) * (1.0 + 2.0 * slab / float(n_slab - 1))
    scaled = jnp.sqrt(err * (ens - 1.0))
    anom = (full - ybar) / scaled
    part = (hxs[pl.ds(pl.multiple_of(share * core, 8), share)] - ybar) / scaled
    dev = (jnp.concatenate([gval[0, 0], gval[1, 0]], axis=1) - ybar) / jnp.sqrt(err)
    both = jnp.concatenate([part, jnp.broadcast_to(dev, (16, 2 * n_obs))], axis=0)
    high, low = halves(anom)
    sums = lax.dot_general(
        left_parts(both), jnp.concatenate([high, low, high], axis=1), (((1,), (1,)), ((), ())),
        preferred_element_type=jnp.float32,
    )
    gpart[...] = sums[: share + 8]

    def p_copy(k):
        tq = lax.rem(q + k, n_pair)
        return remote(gpart, precv.at[q], p_send.at[tq], p_recv.at[q], device(tq, y, m))

    def p_wait(k):
        tq = lax.rem(q + k, n_pair)
        return remote(gpart, precv.at[tq], p_send.at[tq], p_recv.at[tq], device(tq, y, m))

    for k in range(2, n_pair - 1):
        if k > 2:
            stage_tell(k)
        stage_wait(k)
    for k in range(1, n_pair):
        p_copy(k).start()
    precv[q] = sums[: share + 8]
    for k in range(1, n_pair):
        p_wait(k).wait_recv()
    total = precv[0]
    for k in range(1, n_pair):
        total = total + precv[k]
    own = pl.ds(pl.multiple_of(share * core, 8), share)
    theirs = pl.ds(pl.multiple_of(share * (1 - core), 8), share)
    gfull[own] = total[:share]
    g_copy = remote(gfull.at[own], gfull.at[own], g_send, g_recv, device(q, y, sibling))
    g_copy.start()
    proj = jnp.concatenate([total[share:], total[share:]], axis=0)
    remote(gfull.at[theirs], gfull.at[theirs], g_send, g_recv, device(q, y, sibling)).wait_recv()

    ident = jnp.where(
        lax.broadcasted_iota(jnp.int32, (ens, ens), 0) == lax.broadcasted_iota(jnp.int32, (ens, ens), 1), 1.0, 0.0
    )
    matrix = ident + gfull[...]
    scale = jnp.sum(jnp.sum(matrix * ident, axis=1, keepdims=True), axis=0, keepdims=True)

    upper = matrix / scale
    factor = 1.5 * ident - 0.5 * upper
    upper, lower = dot(upper, factor), factor
    for turn in range(ROOT_ITERATIONS - 1):
        factor = 1.5 * ident - 0.5 * dot(lower, upper)
        if turn < ROOT_ITERATIONS - 2:
            upper = dot(upper, factor)
        lower = dot(factor, lower)
    high, low = halves(proj)
    once = lax.dot_general(
        left_parts(lower), jnp.concatenate([high, low, high], axis=1), (((1,), (1,)), ((), ())),
        preferred_element_type=jnp.float32,
    )
    mean_w = dot(lower, once)[:, :1] / (scale * jnp.sqrt(jnp.float32(ens - 1.0)))
    total_w = lower / jnp.sqrt(scale) + mean_w
    omega = 1.0 / ens + total_w - jnp.sum(total_w, axis=0, keepdims=True) / ens
    turned[...] = omega.T
    weights = left_parts(
        jnp.concatenate(
            [turned[pl.ds(pl.multiple_of(kd * m, 8), kd)], turned[pl.ds(pl.multiple_of(kd * sibling, 8), kd)]], axis=0
        )
    )

    def b_copy(h):
        return remote(
            mixed.at[pl.ds(deep * h, deep)],
            out.at[pl.ds(deep * h, deep), :, pl.ds(pl.multiple_of(half * core, 128), half)],
            b_send.at[h], b_recv.at[h], device(q, y, sibling),
        )

    def b_wait(h):
        return remote(
            mixed.at[pl.ds(deep * h, deep)],
            out.at[pl.ds(deep * h, deep), :, pl.ds(pl.multiple_of(half * (1 - core), 128), half)],
            b_send.at[h], b_recv.at[h], device(q, y, sibling),
        )

    for h in range(PARTS):
        for c in range(octs):
            a_keep(c, h).wait()
            for k in range(1, n_group):
                a_wait(c, h, *peer(k)).wait_recv()
        for row in range(deep * h, deep * h + deep):
            result = product(weights, right_parts(fore[row]))
            mixed[row] = result[kd:]
            out[row, :, pl.ds(pl.multiple_of(half * core, 128), half)] = result[:kd]
        b_copy(h).start()

    for f in range(2):
        geo_pair(f).wait_send()
    for f in range(3):
        obs_copy(f).wait_send()
    for c in range(octs):
        for h in range(SPLIT):
            y_copy(c, h).wait_send()

    @pl.when(forward_edge)
    def _():
        for f in range(2):
            geo_direct(f).wait_send()
        for c in range(octs):
            direct_copy(c).wait_send()

    @pl.when(backward_edge)
    def _():
        for f in range(2):
            geo_relay(f).wait_send()
        for c in range(octs):
            for h in range(SPLIT):
                relay_copy(c, h).wait_send()

    for k in range(1, n_group):
        for c in range(octs):
            for h in range(PARTS):
                a_copy(c, h, *peer(k)).wait_send()
        h_copy(*peer(k)).wait_send()
    for k in range(1, n_pair):
        p_copy(k).wait_send()
    g_copy.wait_send()
    for h in range(PARTS):
        b_copy(h).wait_send()
        b_wait(h).wait_recv()


def local(n_slab, n_mem, states, land_mask, cell_class, kappa, flow, obs_index, obs_values, obs_var):
    kd, rows, lon = states.shape
    ens = kd * n_mem
    n_pair, n_group, octs = n_slab // 2, 2 * n_mem, kd // 16
    n_obs = obs_index.shape[0]
    dma = pltpu.SemaphoreType.DMA
    vmem = pl.BlockSpec(memory_space=pltpu.VMEM)
    hbm = pl.BlockSpec(memory_space=pltpu.HBM)
    f32 = jnp.float32
    out = pl.pallas_call(
        functools.partial(cycle_kernel, n_slab, n_mem),
        out_shape=jax.ShapeDtypeStruct((rows, kd, lon), f32),
        in_specs=[hbm] * 8,
        out_specs=vmem,
        scratch_shapes=[
            pltpu.VMEM((2 * octs, 8, rows, lon), f32),
            pltpu.VMEM((octs, rows, 8, lon), f32),
            pltpu.SMEM(kappa.shape, f32),
            pltpu.SMEM(flow.shape, f32),
            pltpu.SemaphoreType.REGULAR((2,)), pltpu.SemaphoreType.REGULAR((n_pair,)), pltpu.SemaphoreType.REGULAR((n_pair,)),
            dma((2 * octs,)), dma((2,)), dma((5,)),
            pltpu.VMEM((octs, 4 * rows, 8, lon), f32),
            pltpu.VMEM((octs, 4 * rows, 8, lon), f32),
            pltpu.VMEM((octs, 4 * rows, 8, lon), f32),
            pltpu.VMEM((4 * rows, 5, 8, lon), f32),
            pltpu.VMEM((4, 2, rows, lon), jnp.int32),
            pltpu.VMEM((2, 1, n_obs), jnp.int32),
            pltpu.VMEM((2, 2, 1, n_obs), f32),
            pltpu.VMEM((lon, 2 * n_obs), jnp.bfloat16),
            pltpu.VMEM((ens, 2 * n_obs), f32),
            pltpu.VMEM((ens // 2 + 8, ens), f32),
            pltpu.VMEM((n_pair, ens // 2 + 8, ens), f32),
            pltpu.VMEM((ens, ens), f32),
            pltpu.VMEM((ens, ens), f32),
            pltpu.VMEM((rows, ens, lon // 2), f32),
            pltpu.VMEM((rows, kd, lon // 2), f32),
            dma((3, 2)), dma((4, 2)), dma((3,)), dma((3,)), dma((octs, SPLIT)), dma((octs, SPLIT)),
            dma((octs,)), dma((octs,)), dma((octs, SPLIT)), dma((octs, SPLIT)), dma((octs,)),
            dma((n_group,)), dma((n_group,)), dma((n_pair,)), dma((n_pair,)), dma, dma,
            dma((octs, PARTS, n_group)), dma((octs, PARTS, n_group)), dma((PARTS,)), dma((PARTS,)),
        ],
        compiler_params=pltpu.CompilerParams(
            collective_id=0, has_side_effects=True, vmem_limit_bytes=48 * 1024 * 1024
        ),
        name="cycle",
    )(
        *(
            pltpu.with_memory_space_constraint(array, pltpu.HBM)
            for array in (
                states, cell_class, land_mask, kappa, flow,
                obs_index.reshape(1, n_obs), obs_values.reshape(1, n_obs), obs_var.reshape(1, n_obs),
            )
        )
    )
    return out.transpose(1, 0, 2)


def solution(mesh):
    return jax.shard_map(
        functools.partial(local, mesh.shape["slab"], mesh.shape["mem"]),
        mesh=mesh,
        in_specs=(
            P("mem", "slab", None),
            P("slab", None),
            P("slab", None),
            P(),
            P(),
            P("slab"),
            P("slab"),
            P("slab"),
        ),
        out_specs=P("mem", "slab", None),
        check_vma=False,
    )
```
